768 devices in a mesh: section: 48 (over x_lo, z, core), rows: 16 (over y, x_hi).
Axes of the slice: x: 4 (x_hi: 2, x_lo: 2; x = x_hi * 2 + x_lo), y: 8, z: 12, core: 2. Of those that a mesh axis runs over, the one named last changes fastest.
Arguments:
- activations: bfloat16 [48, 64, 32, 768], P('section', 'rows'), may hold values from -6 to 6
- cotangent: bfloat16 [48, 64, 32, 3072], P('section', None, None, 'rows'), may hold values from -6 to 6
- proj_weight: bfloat16 [768, 3072], P('section', 'rows'), may hold values from -0.21875 to 0.21875
- kernel_taps: bfloat16 [49, 768], replicated, may hold values from -0.875 to 0.875
- ln_gain: float32 [768], replicated, may hold values from 0.1 to 1.9
- ln_shift: float32 [768], replicated, may hold values from -3 to 3
- heights: int32 [48], P('section'), may hold values from 32 to 64, as said below
- widths: int32 [48], P('section'), may hold values from 16 to 32, as said below
Outputs:
- input_grad: bfloat16 [48, 64, 32, 768], P('section', 'rows')
- weight_grad: float32 [768, 3072], P('section', 'rows')
The draws below stay inside these ranges and needn't reach their ends.
Inputs may be any that keep to these rules, and one draw needn't show every extreme that they name: `heights`: every image has at least half of 64 valid rows, and some image has all 64. `widths`: every image has at least half of 32 valid columns, and some image has all 32.
All inputs are finite; a program needn't handle non-finite values.
Results may differ from the reference program's by a relative error of at most 0.0049.
Values may be sent and summed in bfloat16 or wider, within the bound.
A program may use at most 32 MiB of HBM per device.

```python
import jax
import jax.numpy as jnp
from jax import lax

C = 768
HID = 3072
KS = 7
WID = 32
HEIGHT = 64
IMAGES = 48


def draw_heights(key, part):
    first_key = jax.random.fold_in(key, 11)
    second_key = jax.random.fold_in(key, 12)
    values = jax.random.randint(first_key, (IMAGES,), HEIGHT // 2, HEIGHT + 1)
    chosen = jax.random.randint(second_key, (), 0, IMAGES)
    return jnp.where(jnp.arange(IMAGES) == chosen, HEIGHT, values).astype(jnp.int32)


def draw_widths(key, part):
    first_key = jax.random.fold_in(key, 21)
    second_key = jax.random.fold_in(key, 22)
    values = jax.random.randint(first_key, (IMAGES,), WID // 2, WID + 1)
    chosen = jax.random.randint(second_key, (), 0, IMAGES)
    return jnp.where(jnp.arange(IMAGES) == chosen, WID, values).astype(jnp.int32)


def block_levels(key, dims, pieces, least, top_value):
    factor_of = 1.0
    for dim, blocks in pieces:
        steps = jax.random.uniform(jax.random.fold_in(jax.random.fold_in(key, 6), dim), (blocks,), jnp.float32, least / len(pieces), top_value / len(pieces))
        factor_of = factor_of * jnp.repeat(jnp.exp(steps), dims[dim] // blocks).reshape((-1,) + (1,) * (len(dims) - 1 - dim))
    return factor_of


def gaussian(own_key, dims, width, reach, split=(), dtype=jnp.bfloat16):
    values = jax.random.normal(own_key, dims, jnp.float32) * width
    if len(split) > 0:
        values = block_levels(own_key, dims, split, -0.22, 0.18) * values
    return jnp.clip(values, min=-reach, max=reach).astype(dtype)


def setup_inputs(seed: int = 0) -> dict:
    key_list = jax.random.split(jax.random.key(seed), 9)
    return {
        "activations": gaussian(key_list[0], (IMAGES, HEIGHT, WID, C), 1.0, 6.0, ((0, 48), (1, 16))),
        "cotangent": gaussian(key_list[1], (IMAGES, HEIGHT, WID, HID), 1.0, 6.0, ((0, 48), (3, 16))),
        "proj_weight": gaussian(key_list[2], (C, HID), C ** -0.5, 0.21875, ((0, 48), (1, 16))),
        "kernel_taps": gaussian(key_list[3], (KS * KS, C), (KS * KS) ** -0.5, 0.875),
        "ln_gain": jnp.clip(1.0 + 0.18 * jax.random.normal(key_list[4], (C,), jnp.float32), 0.1, 1.9),
        "ln_shift": gaussian(key_list[5], (C,), 0.5, 3.0, (), jnp.float32),
        "heights": draw_heights(jax.random.fold_in(key_list[8], 71), 0),
        "widths": draw_widths(jax.random.fold_in(key_list[8], 71), 0),
    }


epsilon = 1e-06

def depth_conv(source, weights):
    padded = jnp.pad(source, ((3, 3), (3, 3), (0, 0)))
    height_all = source.shape[0]
    width_all = source.shape[1]
    running = jnp.zeros(source.shape, jnp.float32)
    for across in range(7):
        for along in range(7):
            running = running + weights[across * 7 + along] * padded[across:across + height_all, along:along + width_all]
    return running

def reference(activations, cotangent, proj_weight, kernel_taps, ln_gain, ln_shift, heights, widths):
    row_ids = lax.broadcasted_iota(jnp.int32, (HEIGHT, WID), 0)
    col_ids = lax.broadcasted_iota(jnp.int32, (HEIGHT, WID), 1)
    weights = kernel_taps.astype(jnp.float32)

    def one_image(summed, sample):
        image, grad_in, height_one, width_one = sample
        valid = ((row_ids < height_one) & (col_ids < width_one)).astype(jnp.float32)[:, :, None]
        masked = image.astype(jnp.float32) * valid
        mixed = depth_conv(masked, weights)
        centre = lax.optimization_barrier(jnp.mean(mixed, axis=-1, keepdims=True))
        variance = lax.optimization_barrier(jnp.mean((mixed - centre) ** 2, axis=-1, keepdims=True))
        inv_spread = 1.0 / jnp.sqrt(variance + epsilon)
        unit = (mixed - centre) * inv_spread
        normed = (unit * ln_gain + ln_shift).astype(jnp.bfloat16)
        live_grad = (grad_in.astype(jnp.float32) * valid).astype(jnp.bfloat16)
        normed_flat = normed.reshape(-1, C)
        grad_flat = live_grad.reshape(-1, HID)
        partial_value = jnp.dot(normed_flat.T, grad_flat, preferred_element_type=jnp.float32)
        grad_norm = jnp.dot(grad_flat, proj_weight.T, preferred_element_type=jnp.float32).reshape(HEIGHT, WID, C)
        scaled = grad_norm * ln_gain
        grad_mixed = inv_spread * (scaled - lax.optimization_barrier(jnp.mean(scaled, axis=-1, keepdims=True)) - unit * lax.optimization_barrier(jnp.mean(scaled * unit, axis=-1, keepdims=True)))
        grad_mixed = grad_mixed.astype(jnp.bfloat16).astype(jnp.float32)
        back = depth_conv(grad_mixed, weights[::-1]) * valid
        return (summed + partial_value, back.astype(jnp.bfloat16))
    summed, input_grad = lax.scan(one_image, jnp.zeros((C, HID), jnp.float32), (activations, cotangent, heights, widths))
    return (input_grad, summed / IMAGES)
```

```python
import functools

import jax
import jax.numpy as jnp
from jax import lax
from jax.experimental import pallas as pl
from jax.experimental.pallas import tpu as pltpu
from jax.sharding import PartitionSpec as P

EPS = 1e-06
BF = jnp.bfloat16
F32 = jnp.float32
LANE = 128


class Slots:
    def __init__(self):
        self.count = 0

    def take(self, n=1):
        first = self.count
        self.count += n
        return first


def kernel_body(
    ny, nz, images,
    h_ref, w_ref, act, g_a, g_b, wq, taps, gain, shift,
    ig, wg,
    actx, xp, tf, mx, inv, nrm, gm, gb, ws1, wall, wgp, r1, sp, sm, rp, rm,
    tot, r3, f4, r4, gnp, gns, gnr, gmx, ssem, rsem, lsem,
):
    s = lax.axis_index("section")
    r = lax.axis_index("rows")
    core = lax.rem(s, 2)
    z = lax.rem(lax.div(s, 2), nz)
    xl = lax.div(s, 2 * nz)
    y = lax.div(r, 2)
    xh = lax.rem(r, 2)
    width, chans = act.shape[1], act.shape[2]
    chunks = chans // LANE
    height_all = 8 * ny
    plus, minus = (nz - 1) // 2, nz // 2

    def sec(xl_, z_, c_):
        return (xl_ * nz + z_) * 2 + c_

    def yat(k):
        return lax.rem(y + k + ny, ny)

    def zat(k):
        return lax.rem(z + k + 2 * nz, nz)

    def row(y_, xh_):
        return y_ * 2 + xh_

    slots = Slots()
    started = []

    def send(src, dst, recv, s_, r_, ssem_id=None):
        sid = slots.take()
        cp = pltpu.make_async_remote_copy(
            src_ref=src, dst_ref=dst, send_sem=ssem.at[sid], recv_sem=rsem.at[recv],
            device_id={"section": s_, "rows": r_}, device_id_type=pl.DeviceIdType.MESH,
        )
        cp.start()
        started.append(cp)
        return cp

    recvs = Slots()
    core_s = sec(xl, z, 1 - core)
    xlp_s = sec(1 - xl, z, core)
    zp_s = sec(xl, zat(1), core)
    zm_s = sec(xl, zat(-1), core)

    barrier = pltpu.get_barrier_semaphore()
    peers = [(s, row(yat(k), xh)) for k in range(1, ny)]
    peers += [(s, row(y, 1 - xh)), (s, row(yat(1), 1 - xh)), (s, row(yat(-1), 1 - xh))]
    peers += [(core_s, r), (xlp_s, r), (zp_s, r), (zm_s, r)]
    for s_, r_ in peers:
        pl.semaphore_signal(
            barrier, inc=1, device_id={"section": s_, "rows": r_},
            device_id_type=pl.DeviceIdType.MESH,
        )
    pl.semaphore_wait(barrier, len(peers))

    a_pair, a_halo = recvs.take(), recvs.take(2)
    act_cp = [send(act, actx.at[pl.ds(3 + 4 * xh, 4)], a_pair, s, row(y, 1 - xh))]
    halo_y = yat(2 * xh - 1)
    for to in range(2):
        act_cp.append(
            send(act.at[pl.ds(xh, 3)], actx.at[pl.ds(11 * (1 - xh), 3)], a_halo + xh, s, row(halo_y, to))
        )
    own_act = pltpu.make_async_copy(act, actx.at[pl.ds(3 + 4 * xh, 4)], lsem.at[0])
    own_act.start()

    w1 = recvs.take(ny)
    w1_cp = [send(wq, ws1.at[y], w1 + k, s, row(yat(k), xh)) for k in range(1, ny)]

    ga_id, gb_id = recvs.take(ny), recvs.take(ny)
    g_cp = []
    order = sorted(range(1, ny), key=lambda k: -min(k, ny - k))
    for k in order:
        g_cp.append(send(g_a.at[yat(k)], gm.at[y], ga_id + k, s, row(yat(k), xh)))
        g_cp.append(send(g_b.at[yat(k)], gb.at[y], gb_id + k, s, row(yat(k), xh)))
    own_ga = pltpu.make_async_copy(g_a.at[y], gm.at[y], lsem.at[1])
    own_gb = pltpu.make_async_copy(g_b.at[y], gb.at[y], lsem.at[2])
    own_ga.start()
    own_gb.start()

    ws1[y] = wq[...]
    tf[pl.ds(0, 49), :] = taps[...].astype(F32)
    xp[...] = jnp.zeros_like(xp)

    for cp in w1_cp:
        cp.wait_recv()
    for k in range(ny):
        wall[s, :, k * LANE:(k + 1) * LANE] = ws1[k, :, 0:LANE]
    for k in range(ny // 2):
        wall[s, :, (ny + k) * LANE:(ny + k + 1) * LANE] = ws1[2 * k, :, LANE:] + ws1[2 * k + 1, :, LANE:]

    w2 = recvs.take()
    wp_id, wm_id, wc_id = recvs.take(2 * plus), recvs.take(2 * minus), recvs.take(2 * nz)
    wc_cp = []

    def wblock(sub, z_):
        xl_ = xl if sub == 0 else 1 - xl
        return wall.at[sec(xl_, z_, core)]

    def to_core(sub, z_):
        blk = wblock(sub, z_)
        wc_cp.append(send(blk, blk, wc_id + len(wc_cp), core_s, r))

    wp_cp, wm_cp = {}, {}

    def ring_w(t, sub):
        if t < plus:
            blk = wblock(sub, zat(-t))
            wp_cp[t, sub] = send(blk, blk, wp_id + 2 * t + sub, zp_s, r)
        if t < minus:
            blk = wblock(sub, zat(t))
            wm_cp[t, sub] = send(blk, blk, wm_id + 2 * t + sub, zm_s, r)

    ring_w(0, 0)
    x2 = send(wall.at[s], wall.at[s], w2, xlp_s, r)
    to_core(0, z)

    def ring_w_open():
        x2.wait_recv()
        ring_w(0, 1)
        to_core(1, z)

    def ring_w_step(t):
        for sub in range(2):
            if t <= plus:
                wp_cp[t - 1, sub].wait_recv()
            wm_cp[t - 1, sub].wait_recv()
            ring_w(t, sub)
            if t <= plus:
                to_core(sub, zat(-t))
            to_core(sub, zat(t))

    height, wid = h_ref[0], w_ref[0]
    col_ids = lax.broadcasted_iota(jnp.int32, (width, chans), 0)

    def conv(base, rows_out, flip, lane, put):
        lanes = pl.ds(pl.multiple_of(lane * LANE, LANE), LANE)
        total = [None] * rows_out
        for along in range(7):
            taps_here = []
            for across in range(7):
                i = across * 7 + along
                taps_here.append(tf[pl.ds(48 - i if flip else i, 1), lanes])
            for rho in range(rows_out + 6):
                x = xp[base + rho, 5 + along:5 + along + width, lanes]
                for out in range(max(0, rho - 6), min(rows_out, rho + 1)):
                    term = taps_here[rho - out] * x
                    total[out] = term if total[out] is None else total[out] + term
        for out in range(rows_out):
            put(out, lanes, total[out])

    for cp in act_cp[:1]:
        cp.wait_recv()
    for i in range(2):
        pltpu.make_async_remote_copy(
            src_ref=act.at[pl.ds(xh, 3)], dst_ref=actx.at[pl.ds(11 * (1 - i), 3)],
            send_sem=ssem.at[0], recv_sem=rsem.at[a_halo + i],
            device_id={"section": s, "rows": row(halo_y, 0)}, device_id_type=pl.DeviceIdType.MESH,
        ).wait_recv()
    own_act.wait()

    def expand(i, carry):
        line = 8 * y - 3 + i
        ok = (col_ids < wid) & (line >= 0) & (line < height)
        xp[i, 8:8 + width, :] = jnp.where(ok, actx[i].astype(F32), 0.0)
        return carry

    lax.fori_loop(0, 14, expand, 0)

    ring_w_open()

    def put_mixed(out, lanes, value):
        mx[pl.ds(out * width, width), lanes] = value

    def conv_fwd(lane, carry):
        conv(0, 8, False, lane, put_mixed)
        return carry

    lax.fori_loop(0, chunks // 2, conv_fwd, 0)
    ring_w_step(1)
    lax.fori_loop(chunks // 2, chunks, conv_fwd, 0)
    ring_w_step(2)

    def norm(i, carry):
        px = pl.ds(pl.multiple_of(i * width, width), width)
        x = mx[px, :]
        centre = jnp.mean(x, axis=-1, keepdims=True)
        dev = x - centre
        inv_spread = 1.0 / jnp.sqrt(jnp.mean(dev * dev, axis=-1, keepdims=True) + EPS)
        unit = dev * inv_spread
        mx[px, :] = unit
        inv[px, :] = jnp.broadcast_to(inv_spread, (width, LANE))
        nrm[px, :] = (unit * gain[...] + shift[...]).astype(BF)
        return carry

    lax.fori_loop(0, 8, norm, 0)
    for t in range(3, minus + 1):
        ring_w_step(t)

    for cp in g_cp:
        cp.wait_recv()
    own_ga.wait()
    own_gb.wait()
    half = gb.shape[1]
    low = lax.broadcasted_iota(jnp.int32, (half, LANE), 1) < LANE // 2
    for k in range(ny // 2):
        even, odd = gb[2 * k].astype(F32), gb[2 * k + 1].astype(F32)
        gm[ny + k, 0:half, :] = jnp.where(low, even, pltpu.roll(odd, LANE // 2, 1)).astype(BF)
        gm[ny + k, half:2 * half, :] = jnp.where(low, pltpu.roll(even, LANE // 2, 1), odd).astype(BF)

    blocks = gm.shape[0]

    def weight_part(j, carry):
        g2 = jnp.concatenate([gm[2 * j], gm[2 * j + 1]], axis=1)
        lanes = pl.ds(pl.multiple_of(j * 2 * LANE, 2 * LANE), 2 * LANE)
        for i in range(chans // 256):
            part = lax.dot_general(
                nrm[:, i * 256:(i + 1) * 256], g2, (((0,), (0,)), ((), ())), preferred_element_type=F32
            )
            wgp[8 * i:8 * i + 8, :, :, lanes] = part.astype(BF).reshape(8, 2, 16, 2 * LANE)
        return carry

    lax.fori_loop(0, blocks // 2, weight_part, 0)
    r1_id = recvs.take()
    r1_cp = send(wgp.at[:, 1 - core], r1, r1_id, core_s, r)

    for cp in wc_cp:
        cp.wait_recv()

    def grad_part(i, carry):
        here = wall[pl.ds(i * 16, 16)].reshape(256, blocks * LANE)
        value = jnp.zeros((gm.shape[1], 256), F32)
        for j in range(blocks // 2):
            g2 = jnp.concatenate([gm[2 * j], gm[2 * j + 1]], axis=1)
            value = value + lax.dot_general(
                g2, here[:, j * 256:(j + 1) * 256], (((1,), (1,)), ((), ())), preferred_element_type=F32
            )
        lanes = pl.ds(pl.multiple_of(i * 256, 256), 256)
        gnp[:, lanes] = value
        gns[:, lanes] = value.astype(BF)
        return carry

    lax.fori_loop(0, chans // 256, grad_part, 0)
    gn_id = recvs.take()
    gn_cp = send(gns, gnr, gn_id, s, row(y, 1 - xh))

    r1_cp.wait_recv()
    rp_id, rm_id = recvs.take(2 * plus), recvs.take(2 * minus)

    def local_sum(sub, z_):
        at = sub * nz + z_
        return wgp[at, core].astype(F32) + r1[at].astype(F32)

    rp_cp, rm_cp = {}, {}

    def ring_r(t):
        for sub in range(2):
            if t < minus:
                value = local_sum(sub, zat(t - minus))
                if t > 0:
                    rm_cp[t - 1, sub].wait_recv()
                    value = value + rm[t - 1, sub].astype(F32)
                sm[t, sub] = value.astype(BF)
                rm_cp[t, sub] = send(sm.at[t, sub], rm.at[t, sub], rm_id + 2 * t + sub, zm_s, r)
            if t < plus:
                value = local_sum(sub, zat(plus - t))
                if t > 0:
                    rp_cp[t - 1, sub].wait_recv()
                    value = value + rp[t - 1, sub].astype(F32)
                sp[t, sub] = value.astype(BF)
                rp_cp[t, sub] = send(sp.at[t, sub], rp.at[t, sub], rp_id + 2 * t + sub, zp_s, r)

    ring_r(0)
    ring_r(1)

    gn_cp.wait_recv()

    def norm_back(i, carry):
        px = pl.ds(pl.multiple_of(i * width, width), width)
        scaled = (gnp[px, :] + gnr[px, :].astype(F32)) * gain[...]
        unit = mx[px, :]
        first = jnp.mean(scaled, axis=-1, keepdims=True)
        second = jnp.mean(scaled * unit, axis=-1, keepdims=True)
        gmx[3 + i] = (inv[px, 0:1] * (scaled - first - unit * second)).astype(BF)
        return carry

    lax.fori_loop(0, 8, norm_back, 0)
    hb_id = recvs.take()
    hb_cp = send(
        gmx.at[pl.ds(8 - 5 * xh, 3)], gmx.at[pl.ds(11 * xh, 3)], hb_id, s, row(yat(1 - 2 * xh), xh)
    )
    ring_r(2)
    hb_cp.wait_recv()

    def expand_back(i, carry):
        at = 4 * xh + i
        line = 8 * y - 3 + at
        ok = (line >= 0) & (line < height_all) & (col_ids >= 0)
        xp[i, 8:8 + width, :] = jnp.where(ok, gmx[at].astype(F32), 0.0)
        return carry

    lax.fori_loop(0, 10, expand_back, 0)
    out_cols = lax.broadcasted_iota(jnp.int32, (width, LANE), 0)

    def put_out(out, lanes, value):
        ok = (out_cols < wid) & (8 * y + 4 * xh + out < height)
        ig[out, :, lanes] = jnp.where(ok, value, 0.0).astype(BF)

    def conv_back(lane, carry):
        conv(0, 4, True, lane, put_out)
        return carry

    lax.fori_loop(0, chunks // 2, conv_back, 0)
    ring_r(3)
    lax.fori_loop(chunks // 2, chunks, conv_back, 0)
    for t in range(4, minus):
        ring_r(t)
    for sub in range(2):
        rm_cp[minus - 1, sub].wait_recv()
        rp_cp[plus - 1, sub].wait_recv()
        tot[sub] = local_sum(sub, z) + rm[minus - 1, sub].astype(F32) + rp[plus - 1, sub].astype(F32)

    r3_id = recvs.take()
    r3_cp = send(tot.at[1 - xl], r3, r3_id, xlp_s, r)
    r3_cp.wait_recv()
    done = tot[xl] + r3[...]
    for k in range(ny):
        f4[k, 0] = done[:, k * LANE:(k + 1) * LANE]
        at = ny + k // 2
        f4[k, 1] = done[:, at * LANE:(at + 1) * LANE]
    r4_id = recvs.take(ny)
    r4_cp = [send(f4.at[yat(k)], r4.at[y], r4_id + k, s, row(yat(k), xh)) for k in range(1, ny)]
    for cp in r4_cp:
        cp.wait_recv()
    r4[y] = f4[y]
    total = r4[0]
    for k in range(1, ny):
        total = total + r4[k]
    tail = jnp.where(lax.rem(y, 2) == 0, total[1], pltpu.roll(total[1], LANE // 2, 1))
    wg[:, 0:LANE] = total[0] / images
    wg[:, LANE:] = tail[:, 0:LANE // 2] / images

    for cp in started:
        cp.wait_send()
    assert slots.count <= ssem.shape[0] and recvs.count <= rsem.shape[0]


def local(ny, nz, images, activations, cotangent, proj_weight, kernel_taps, ln_gain, ln_shift, heights, widths):
    rows_dev, width, chans = activations.shape[1:]
    height_all, hidden = cotangent.shape[1], cotangent.shape[3]
    blocks = ny + ny // 2
    px = 2 * rows_dev * width
    row_ids = lax.broadcasted_iota(jnp.int32, (height_all, width), 0)
    col_ids = lax.broadcasted_iota(jnp.int32, (height_all, width), 1)
    valid = (row_ids < heights[0]) & (col_ids < widths[0])
    live = jnp.where(valid[:, :, None], cotangent[0], jnp.zeros((), BF))
    g_a = live[:, :, :LANE].reshape(ny, px, LANE)
    tail = live[:, :, LANE:].reshape(ny, 2, px // 2, hidden - LANE)
    g_b = jnp.concatenate([tail[:, 0], tail[:, 1]], axis=-1)
    odd = lax.rem(lax.div(lax.axis_index("rows"), 2), 2) == 1
    w_tail = proj_weight[:, LANE:]
    w_none = jnp.zeros_like(w_tail)
    wq = jnp.concatenate(
        [proj_weight[:, :LANE], jnp.where(odd, w_none, w_tail), jnp.where(odd, w_tail, w_none)], axis=-1
    )
    plus, minus = (nz - 1) // 2, nz // 2
    cols = blocks * LANE
    vmem = pltpu.VMEM
    out = pl.pallas_call(
        functools.partial(kernel_body, ny, nz, float(images)),
        out_shape=(
            jax.ShapeDtypeStruct((rows_dev, width, chans), BF),
            jax.ShapeDtypeStruct((16, hidden), F32),
        ),
        in_specs=[pl.BlockSpec(memory_space=pltpu.SMEM)] * 2
        + [pl.BlockSpec(memory_space=pl.ANY)] * 3
        + [pl.BlockSpec(memory_space=vmem)] * 4,
        out_specs=[pl.BlockSpec(memory_space=vmem)] * 2,
        scratch_shapes=[
            vmem((14, width, chans), BF),
            vmem((14, width + 16, chans), F32),
            vmem((56, chans), F32),
            vmem((px, chans), F32),
            vmem((px, LANE), F32),
            vmem((px, chans), BF),
            vmem((blocks, px, LANE), BF),
            vmem((ny, px // 2, LANE), BF),
            vmem((ny, 16, 2 * LANE), BF),
            vmem((4 * nz, 16, cols), BF),
            vmem((2 * nz, 2, 16, cols), BF),
            vmem((2 * nz, 16, cols), BF),
            vmem((plus, 2, 16, cols), BF),
            vmem((minus, 2, 16, cols), BF),
            vmem((plus, 2, 16, cols), BF),
            vmem((minus, 2, 16, cols), BF),
            vmem((2, 16, cols), F32),
            vmem((16, cols), F32),
            vmem((ny, 2, 16, LANE), F32),
            vmem((ny, 2, 16, LANE), F32),
            vmem((px, chans), F32),
            vmem((px, chans), BF),
            vmem((px, chans), BF),
            vmem((14, width, chans), BF),
            pltpu.SemaphoreType.DMA((160,)),
            pltpu.SemaphoreType.DMA((160,)),
            pltpu.SemaphoreType.DMA((3,)),
        ],
        compiler_params=pltpu.CompilerParams(
            collective_id=0, has_side_effects=True, vmem_limit_bytes=60 * 1024 * 1024
        ),
    )(
        heights, widths, activations[0], g_a, g_b, wq, kernel_taps,
        ln_gain.reshape(1, chans), ln_shift.reshape(1, chans),
    )
    return out[0][None], out[1]


def solution(mesh):
    ny = mesh.shape["rows"] // 2
    nz = mesh.shape["section"] // 4
    in_specs = (
        P("section", "rows", None, None),
        P("section", None, None, "rows"),
        P("section", "rows"),
        P(),
        P(),
        P(),
        P("section"),
        P("section"),
    )
    out_specs = (P("section", "rows", None, None), P("section", "rows"))
    body = functools.partial(local, ny, nz, mesh.shape["section"])
    return jax.shard_map(body, mesh=mesh, in_specs=in_specs, out_specs=out_specs, check_vma=False)
```

```python
import functools

import jax
import jax.numpy as jnp
from jax import lax
from jax.experimental import pallas as pl
from jax.experimental.pallas import tpu as pltpu
from jax.sharding import PartitionSpec as P

EPS = 1e-06
BF = jnp.bfloat16
F32 = jnp.float32
LANE = 128


class Slots:
    def __init__(self):
        self.count = 0

    def take(self, n=1):
        first = self.count
        self.count += n
        return first


def kernel_body(
    ny, nz, images,
    h_ref, w_ref, act, cot, proj, taps, gain, shift,
    ig, wg,
    actx, xp, tf, mx, inv, nrm, cbuf, g_a, g_b, gm, gb, wq, ws1, wall, wgp, r1, sp, sm, rp, rm,
    f4, r4, gnp, gns, gnr, gmx, ssem, rsem, lsem,
):
    s = lax.axis_index("section")
    r = lax.axis_index("rows")
    core = lax.rem(s, 2)
    z = lax.rem(lax.div(s, 2), nz)
    xl = lax.div(s, 2 * nz)
    y = lax.div(r, 2)
    xh = lax.rem(r, 2)
    width, chans = act.shape[1], act.shape[2]
    chunks = chans // LANE
    height_all = cot.shape[0]
    half_px = g_b.shape[1]
    plus, minus = (nz - 1) // 2, nz // 2
    quarter = ny // 2
    per_half = quarter + quarter // 2
    blocks = 2 * per_half
    off = sorted(range(ny), key=lambda k: min(k, ny - k))

    def main_block(p):
        return per_half * (p // quarter) + p % quarter

    def pair_block(p):
        return per_half * (p // quarter) + quarter + (p % quarter) // 2

    def sec(xl_, z_, c_):
        return (xl_ * nz + z_) * 2 + c_

    def yat(k):
        return lax.rem(y + k + ny, ny)

    def zat(k):
        return lax.rem(z + k + 2 * nz, nz)

    def row(y_, xh_):
        return y_ * 2 + xh_

    def lanes_of(i, n=1):
        return slice(i * LANE, (i + n) * LANE)

    slots = Slots()
    recvs = Slots()
    started = []

    def send(src, dst, recv, s_, r_):
        cp = pltpu.make_async_remote_copy(
            src_ref=src, dst_ref=dst, send_sem=ssem.at[slots.take()], recv_sem=rsem.at[recv],
            device_id={"section": s_, "rows": r_}, device_id_type=pl.DeviceIdType.MESH,
        )
        cp.start()
        started.append(cp)
        return cp

    core_s = sec(xl, z, 1 - core)
    xlp_s = sec(1 - xl, z, core)
    zp_s = sec(xl, zat(1), core)
    zm_s = sec(xl, zat(-1), core)

    barrier = pltpu.get_barrier_semaphore()
    peers = [(xs, row(yat(k), xh)) for k in range(ny) for xs in (s, xlp_s) if not (k == 0 and xs is s)]
    peers += [(s, row(y, 1 - xh)), (s, row(yat(1), 1 - xh)), (s, row(yat(-1), 1 - xh))]
    peers += [(core_s, r), (zp_s, r), (zm_s, r)]
    for s_, r_ in peers:
        pl.semaphore_signal(
            barrier, inc=1, device_id={"section": s_, "rows": r_},
            device_id_type=pl.DeviceIdType.MESH,
        )

    own_cot = pltpu.make_async_copy(cot, cbuf, lsem.at[1])
    own_cot.start()
    own_act = pltpu.make_async_copy(act, actx.at[pl.ds(3 + 4 * xh, 4)], lsem.at[0])
    own_act.start()
    wq[:, LANE:] = jnp.zeros((16, LANE), BF)
    wq[:, 0:proj.shape[1]] = proj[...]
    ws1[0] = wq[...]
    tf[pl.ds(0, 49), :] = taps[...].astype(F32)
    xp[...] = jnp.zeros_like(xp)
    height, wid = h_ref[0], w_ref[0]
    own_cot.wait()
    cols3 = lax.broadcasted_iota(jnp.int32, (8, width, LANE), 1)
    rows3 = lax.broadcasted_iota(jnp.int32, (8, width, LANE), 0)
    low = lax.broadcasted_iota(jnp.int32, (half_px, LANE), 1) < LANE // 2

    def pack(i, carry):
        lines = pl.ds(pl.multiple_of(i * 8, 8), 8)
        ok = (cols3 < wid) & (rows3 + i * 8 < height)
        main = jnp.where(ok, cbuf[lines, :, 0:LANE].astype(F32), 0.0)
        g_a[i] = main.astype(BF).reshape(2 * half_px, LANE)
        tail = cbuf[lines, :, LANE:].astype(F32)
        tail = jnp.concatenate([tail, tail], axis=-1)
        tail = jnp.where(ok, tail, 0.0).reshape(2 * half_px, LANE)
        g_b[i] = jnp.where(low, tail[:half_px], tail[half_px:]).astype(BF)
        return carry

    lax.fori_loop(0, ny, pack, 0)
    pl.semaphore_wait(barrier, len(peers))

    w1 = recvs.take(2 * ny)
    w1_cp = []
    for p in range(ny):
        for sub in range(2):
            if p or sub:
                w1_cp.append(
                    send(wq, ws1.at[2 * p + sub], w1 + 2 * p + sub, xlp_s if sub else s, row(yat(-off[p]), xh))
                )

    a_pair, a_halo = recvs.take(), recvs.take(2)
    pair_cp = send(act, actx.at[pl.ds(3 + 4 * xh, 4)], a_pair, s, row(y, 1 - xh))
    halo_y = yat(2 * xh - 1)
    for to in range(2):
        halo_cp = send(
            act.at[pl.ds(xh, 3)], actx.at[pl.ds(11 * (1 - xh), 3)], a_halo + xh, s, row(halo_y, to)
        )

    ga_id, gb_id = recvs.take(ny), recvs.take(ny)
    g_cp = {}
    for p in range(1, ny):
        to = yat(-off[p])
        g_cp[p] = (
            send(g_a.at[to], gm.at[main_block(p)], ga_id + p, s, row(to, xh)),
            send(g_b.at[to], gb.at[p], gb_id + p, s, row(to, xh)),
        )
    own_ga = pltpu.make_async_copy(g_a.at[y], gm.at[0], lsem.at[1])
    own_gb = pltpu.make_async_copy(g_b.at[y], gb.at[0], lsem.at[2])
    own_ga.start()
    own_gb.start()

    wp_id, wm_id, wc_id = recvs.take(2 * plus), recvs.take(2 * minus), recvs.take(2 * nz)
    wc_cp = []
    wp_cp, wm_cp = {}, {}

    def wblock(sub, z_):
        return wall.at[sec(1 - xl if sub else xl, z_, core)]

    def to_core(sub, z_):
        blk = wblock(sub, z_)
        wc_cp.append(send(blk, blk, wc_id + len(wc_cp), core_s, r))

    def ring_w(t, sub):
        if t < plus:
            blk = wblock(sub, zat(-t))
            wp_cp[t, sub] = send(blk, blk, wp_id + 2 * t + sub, zp_s, r)
        if t < minus:
            blk = wblock(sub, zat(t))
            wm_cp[t, sub] = send(blk, blk, wm_id + 2 * t + sub, zm_s, r)

    low16 = lax.broadcasted_iota(jnp.int32, (16, LANE), 1) < LANE // 2

    def ring_w_open():
        for cp in w1_cp:
            cp.wait_recv()
        for sub in range(2):
            at = sec(1 - xl if sub else xl, z, core)
            for p in range(ny):
                wall[at, :, lanes_of(main_block(p))] = ws1[2 * p + sub, :, 0:LANE]
            for p in range(0, ny, 2):
                first = ws1[2 * p + sub, :, LANE:].astype(F32)
                second = ws1[2 * p + 2 + sub, :, LANE:].astype(F32)
                wall[at, :, lanes_of(pair_block(p))] = jnp.where(
                    low16, first, pltpu.roll(second, LANE // 2, 1)
                ).astype(BF)
        for sub in range(2):
            ring_w(0, sub)
        for sub in range(2):
            to_core(sub, z)

    def ring_w_step(t):
        for sub in range(2):
            if t <= plus:
                wp_cp[t - 1, sub].wait_recv()
            wm_cp[t - 1, sub].wait_recv()
            ring_w(t, sub)
            if t <= plus:
                to_core(sub, zat(-t))
            to_core(sub, zat(t))

    col_ids = lax.broadcasted_iota(jnp.int32, (width, chans), 0)

    def conv(rows_out, flip, lane, put):
        lanes = pl.ds(pl.multiple_of(lane * LANE, LANE), LANE)
        total = [None] * rows_out
        for along in range(7):
            taps_here = []
            for across in range(7):
                i = across * 7 + along
                taps_here.append(tf[pl.ds(48 - i if flip else i, 1), lanes])
            for rho in range(rows_out + 6):
                x = xp[rho, 5 + along:5 + along + width, lanes]
                for out in range(max(0, rho - 6), min(rows_out, rho + 1)):
                    term = taps_here[rho - out] * x
                    total[out] = term if total[out] is None else total[out] + term
        for out in range(rows_out):
            put(out, lanes, total[out])

    ring_w_open()
    ring_w_step(1)
    pair_cp.wait_recv()
    for i in range(2):
        pltpu.make_async_remote_copy(
            src_ref=act.at[pl.ds(xh, 3)], dst_ref=actx.at[pl.ds(11 * (1 - i), 3)],
            send_sem=ssem.at[0], recv_sem=rsem.at[a_halo + i],
            device_id={"section": s, "rows": row(halo_y, 0)}, device_id_type=pl.DeviceIdType.MESH,
        ).wait_recv()
    own_act.wait()

    def expand(i, carry):
        line = 8 * y - 3 + i
        ok = (col_ids < wid) & (line >= 0) & (line < height)
        xp[i, 8:8 + width, :] = jnp.where(ok, actx[i].astype(F32), 0.0)
        return carry

    lax.fori_loop(0, 14, expand, 0)

    def put_mixed(out, lanes, value):
        mx[pl.ds(out * width, width), lanes] = value

    def conv_fwd(lane, carry):
        conv(8, False, lane, put_mixed)
        return carry

    lax.fori_loop(0, chunks // 2, conv_fwd, 0)
    ring_w_step(2)
    lax.fori_loop(chunks // 2, chunks, conv_fwd, 0)
    ring_w_step(3)

    def norm(i, carry):
        px = pl.ds(pl.multiple_of(i * width, width), width)
        x = mx[px, :]
        centre = jnp.mean(x, axis=-1, keepdims=True)
        dev = x - centre
        inv_spread = 1.0 / jnp.sqrt(jnp.mean(dev * dev, axis=-1, keepdims=True) + EPS)
        unit = dev * inv_spread
        mx[px, :] = unit
        inv[px, :] = jnp.broadcast_to(inv_spread, (width, LANE))
        nrm[px, :] = (unit * gain[...] + shift[...]).astype(BF)
        return carry

    lax.fori_loop(0, 8, norm, 0)

    r1_id = recvs.take(2)
    r1_cp = {}

    def weight_half(h):
        for p in range(h * quarter, (h + 1) * quarter):
            if p:
                g_cp[p][0].wait_recv()
                g_cp[p][1].wait_recv()
        if h == 0:
            own_ga.wait()
            own_gb.wait()
        for p in range(h * quarter, (h + 1) * quarter, 2):
            first, second = gb[p].astype(F32), gb[p + 1].astype(F32)
            at = pair_block(p)
            gm[at, 0:half_px, :] = jnp.where(low, first, pltpu.roll(second, LANE // 2, 1)).astype(BF)
            gm[at, half_px:, :] = jnp.where(low, pltpu.roll(first, LANE // 2, 1), second).astype(BF)

        def weight_part(j, carry):
            at = h * per_half + 2 * j
            g2 = jnp.concatenate([gm[at], gm[at + 1]], axis=1)
            lanes = pl.ds(pl.multiple_of(j * 2 * LANE, 2 * LANE), 2 * LANE)
            for i in range(chans // 256):
                part = lax.dot_general(
                    nrm[:, i * 256:(i + 1) * 256], g2, (((0,), (0,)), ((), ())), preferred_element_type=F32
                )
                wgp[h, 8 * i:8 * i + 8, :, :, lanes] = part.astype(BF).reshape(8, 2, 16, 2 * LANE)
            return carry

        lax.fori_loop(0, per_half // 2, weight_part, 0)
        r1_cp[h] = send(wgp.at[h, :, 1 - core], r1.at[h], r1_id + h, core_s, r)

    rp_id, rm_id = recvs.take(2 * plus), recvs.take(2 * minus)
    rp_cp, rm_cp = {}, {}

    def local_sum(h, xl_, z_):
        at = xl_ * nz + z_
        return wgp[h, at, core].astype(F32) + r1[h, at].astype(F32)

    def ring_r(t, h):
        if t == 0:
            r1_cp[h].wait_recv()
        if t < minus:
            if t > 0:
                rm_cp[t - 1, h].wait_recv()
            for xl_ in range(2):
                value = local_sum(h, xl_, zat(t - minus))
                if t > 0:
                    value = value + rm[t - 1, h, xl_].astype(F32)
                sm[t, h, xl_] = value.astype(BF)
            rm_cp[t, h] = send(sm.at[t, h], rm.at[t, h], rm_id + 2 * t + h, zm_s, r)
        if t < plus:
            if t > 0:
                rp_cp[t - 1, h].wait_recv()
            for xl_ in range(2):
                value = local_sum(h, xl_, zat(plus - t))
                if t > 0:
                    value = value + rp[t - 1, h, xl_].astype(F32)
                sp[t, h, xl_] = value.astype(BF)
            rp_cp[t, h] = send(sp.at[t, h], rp.at[t, h], rp_id + 2 * t + h, zp_s, r)

    r4_id = recvs.take(4 * ny)
    r4_cp = []

    def finish(h):
        rm_cp[minus - 1, h].wait_recv()
        rp_cp[plus - 1, h].wait_recv()
        for sub in range(2):
            xl_ = 1 - xl if sub else xl
            done = local_sum(h, xl_, z) + rm[minus - 1, h, xl_].astype(F32) + rp[plus - 1, h, xl_].astype(F32)
            for p in range(h * quarter, (h + 1) * quarter):
                f4[2 * p + sub, 0] = done[:, lanes_of(main_block(p) - h * per_half)]
                f4[2 * p + sub, 1] = done[:, lanes_of(pair_block(p) - h * per_half)]
        for p in range(h * quarter, (h + 1) * quarter):
            for sub in range(2):
                if p or sub:
                    at = 2 * p + sub
                    r4_cp.append(
                        send(f4.at[at], r4.at[at], r4_id + at, xlp_s if sub else s, row(yat(off[p]), xh))
                    )

    gn_id = recvs.take(chans // 256)
    gn_cp = []

    def grad_part(i):
        value = jnp.zeros((gm.shape[1], 256), F32)
        for j in range(blocks // 2):
            g2 = jnp.concatenate([gm[2 * j], gm[2 * j + 1]], axis=1)
            here = wall[16 * i:16 * i + 16, :, lanes_of(2 * j, 2)].reshape(256, 256)
            value = value + lax.dot_general(
                g2, here, (((1,), (1,)), ((), ())), preferred_element_type=F32
            )
        gnp[:, 256 * i:256 * i + 256] = value
        gns[i] = value.astype(BF)
        gn_cp.append(send(gns.at[i], gnr.at[i], gn_id + i, s, row(y, 1 - xh)))

    def norm_back(i, carry):
        px = pl.ds(pl.multiple_of(i * width, width), width)
        other = jnp.concatenate([gnr[j, px, :] for j in range(chans // 256)], axis=1)
        scaled = (gnp[px, :] + other.astype(F32)) * gain[...]
        unit = mx[px, :]
        first = jnp.mean(scaled, axis=-1, keepdims=True)
        second = jnp.mean(scaled * unit, axis=-1, keepdims=True)
        gmx[3 + i] = (inv[px, 0:1] * (scaled - first - unit * second)).astype(BF)
        return carry

    def expand_back(i, carry):
        at = 4 * xh + i
        line = 8 * y - 3 + at
        ok = (line >= 0) & (line < height_all) & (col_ids >= 0)
        xp[i, 8:8 + width, :] = jnp.where(ok, gmx[at].astype(F32), 0.0)
        return carry

    out_cols = lax.broadcasted_iota(jnp.int32, (width, LANE), 0)

    def put_out(out, lanes, value):
        ok = (out_cols < wid) & (8 * y + 4 * xh + out < height)
        ig[out, :, lanes] = jnp.where(ok, value, 0.0).astype(BF)

    def conv_back(lane, carry):
        conv(4, True, lane, put_out)
        return carry

    weight_half(0)
    ring_w_step(4)
    ring_r(0, 0)
    weight_half(1)
    ring_w_step(5)
    ring_r(1, 0)
    ring_r(0, 1)
    ring_w_step(6)
    ring_r(2, 0)
    ring_r(1, 1)
    for cp in wc_cp:
        cp.wait_recv()
    for i in range(chans // 256):
        grad_part(i)
    ring_r(3, 0)
    ring_r(2, 1)
    ring_r(4, 0)
    ring_r(3, 1)
    ring_r(5, 0)
    ring_r(4, 1)
    for cp in gn_cp:
        cp.wait_recv()
    lax.fori_loop(0, 8, norm_back, 0)
    hb_id = recvs.take()
    hb_cp = send(
        gmx.at[pl.ds(8 - 5 * xh, 3)], gmx.at[pl.ds(11 * xh, 3)], hb_id, s, row(yat(1 - 2 * xh), xh)
    )
    finish(0)
    ring_r(5, 1)
    finish(1)
    hb_cp.wait_recv()
    lax.fori_loop(0, 10, expand_back, 0)
    lax.fori_loop(0, chunks, conv_back, 0)
    for cp in r4_cp:
        cp.wait_recv()
    r4[0] = f4[0]
    main = r4[0, 0]
    tails = [r4[0, 1], r4[2, 1]]
    for at in range(1, 2 * ny):
        main = main + r4[at, 0]
        if at not in (0, 2):
            tails[(at // 2) % 2] = tails[(at // 2) % 2] + r4[at, 1]
    tail = tails[0] + pltpu.roll(tails[1], LANE // 2, 1)
    wg[:, 0:LANE] = main / images
    wg[:, LANE:] = tail[:, 0:LANE // 2] / images

    for cp in started:
        cp.wait_send()
    assert slots.count <= ssem.shape[0] and recvs.count <= rsem.shape[0]


def local(ny, nz, images, activations, cotangent, proj_weight, kernel_taps, ln_gain, ln_shift, heights, widths):
    rows_dev, width, chans = activations.shape[1:]
    height_all, hidden = cotangent.shape[1], cotangent.shape[3]
    blocks = ny + ny // 2
    px = 2 * rows_dev * width
    plus, minus = (nz - 1) // 2, nz // 2
    cols = blocks * LANE
    vmem = pltpu.VMEM
    out = pl.pallas_call(
        functools.partial(kernel_body, ny, nz, float(images)),
        out_shape=(
            jax.ShapeDtypeStruct((rows_dev, width, chans), BF),
            jax.ShapeDtypeStruct((16, hidden), F32),
        ),
        in_specs=[pl.BlockSpec(memory_space=pltpu.SMEM)] * 2
        + [pl.BlockSpec(memory_space=pl.ANY)] * 2
        + [pl.BlockSpec(memory_space=vmem)] * 4,
        out_specs=[pl.BlockSpec(memory_space=vmem)] * 2,
        scratch_shapes=[
            vmem((14, width, chans), BF),
            vmem((14, width + 16, chans), F32),
            vmem((56, chans), F32),
            vmem((px, chans), F32),
            vmem((px, LANE), F32),
            vmem((px, chans), BF),
            vmem((height_all, width, hidden), BF),
            vmem((ny, px, LANE), BF),
            vmem((ny, px // 2, LANE), BF),
            vmem((blocks, px, LANE), BF),
            vmem((ny, px // 2, LANE), BF),
            vmem((16, 2 * LANE), BF),
            vmem((2 * ny, 16, 2 * LANE), BF),
            vmem((4 * nz, 16, cols), BF),
            vmem((2, 2 * nz, 2, 16, cols // 2), BF),
            vmem((2, 2 * nz, 16, cols // 2), BF),
            vmem((plus, 2, 2, 16, cols // 2), BF),
            vmem((minus, 2, 2, 16, cols // 2), BF),
            vmem((plus, 2, 2, 16, cols // 2), BF),
            vmem((minus, 2, 2, 16, cols // 2), BF),
            vmem((2 * ny, 2, 16, LANE), F32),
            vmem((2 * ny, 2, 16, LANE), F32),
            vmem((px, chans), F32),
            vmem((chans // 256, px, 256), BF),
            vmem((chans // 256, px, 256), BF),
            vmem((14, width, chans), BF),
            pltpu.SemaphoreType.DMA((192,)),
            pltpu.SemaphoreType.DMA((192,)),
            pltpu.SemaphoreType.DMA((3,)),
        ],
        compiler_params=pltpu.CompilerParams(
            collective_id=0, has_side_effects=True, vmem_limit_bytes=60 * 1024 * 1024
        ),
    )(
        heights, widths, activations[0], cotangent[0], proj_weight, kernel_taps,
        ln_gain.reshape(1, chans), ln_shift.reshape(1, chans),
    )
    return out[0][None], out[1]


def solution(mesh):
    ny = mesh.shape["rows"] // 2
    nz = mesh.shape["section"] // 4
    in_specs = (
        P("section", "rows", None, None),
        P("section", None, None, "rows"),
        P("section", "rows"),
        P(),
        P(),
        P(),
        P("section"),
        P("section"),
    )
    out_specs = (P("section", "rows", None, None), P("section", "rows"))
    body = functools.partial(local, ny, nz, mesh.shape["section"])
    return jax.shard_map(body, mesh=mesh, in_specs=in_specs, out_specs=out_specs, check_vma=False)
```

```python
import functools

import jax
import jax.numpy as jnp
from jax import lax
from jax.experimental import pallas as pl
from jax.experimental.pallas import tpu as pltpu
from jax.sharding import PartitionSpec as P

EPS = 1e-06
BF = jnp.bfloat16
F32 = jnp.float32
LANE = 128


class Slots:
    def __init__(self):
        self.count = 0

    def take(self, n=1):
        first = self.count
        self.count += n
        return first


def kernel_body(
    ny, nz, images,
    h_ref, w_ref, act, cot, proj, taps, gain_in, shift_in,
    ig, wg,
    actx, xp, tf, mx, inv, nrm, cbuf, g_a, g_b, gm, gb, wq, ws1, wall, wgp, r1, sp, sm, rp, rm,
    f4, r4, gnp, gns, gnr, gmx, gain, shift, qa_p, qa_m, qh_p, qh_m, qg_p, qg_m, ssem, rsem, lsem,
):
    s = lax.axis_index("section")
    r = lax.axis_index("rows")
    core = lax.rem(s, 2)
    z = lax.rem(lax.div(s, 2), nz)
    xl = lax.div(s, 2 * nz)
    y = lax.div(r, 2)
    xh = lax.rem(r, 2)
    width, chans = act.shape[1], act.shape[2]
    chunks = chans // LANE
    height_all = cot.shape[0]
    half_px = g_b.shape[1]
    plus, minus = (nz - 1) // 2, nz // 2
    quarter = ny // 2
    per_half = quarter + quarter // 2
    blocks = 2 * per_half
    off = sorted(range(ny), key=lambda k: min(k, ny - k))
    own = off.index(0)

    def main_block(p):
        return per_half * (p // quarter) + p % quarter

    def pair_block(p):
        return per_half * (p // quarter) + quarter + (p % quarter) // 2

    def sec(xl_, z_, c_):
        return (xl_ * nz + z_) * 2 + c_

    def yat(k):
        return lax.rem(y + k + ny, ny)

    def zat(k):
        return lax.rem(z + k + 2 * nz, nz)

    def row(y_, xh_):
        return y_ * 2 + xh_

    def lanes_of(i, n=1):
        return slice(i * LANE, (i + n) * LANE)

    slots = Slots()
    recvs = Slots()
    started = []

    def send(src, dst, recv, s_, r_):
        cp = pltpu.make_async_remote_copy(
            src_ref=src, dst_ref=dst, send_sem=ssem.at[slots.take()], recv_sem=rsem.at[recv],
            device_id={"section": s_, "rows": r_}, device_id_type=pl.DeviceIdType.MESH,
        )
        cp.start()
        started.append(cp)
        return cp

    core_s = sec(xl, z, 1 - core)
    xlp_s = sec(1 - xl, z, core)
    xh_p = lax.rem(xh + xl, 2)
    zp_s = sec(xl, zat(1), core)
    zm_s = sec(xl, zat(-1), core)

    barrier = pltpu.get_barrier_semaphore()
    peers = [(xs, row(yat(k), xh)) for k in range(ny) for xs in (s, xlp_s) if not (k == 0 and xs is s)]
    peers += [(xlp_s, row(yat(k), 1 - xh)) for k in (0, 1, -1)]
    peers += [(core_s, r), (zp_s, r), (zm_s, r)]
    for s_, r_ in peers:
        pl.semaphore_signal(
            barrier, inc=1, device_id={"section": s_, "rows": r_},
            device_id_type=pl.DeviceIdType.MESH,
        )

    own_cot = pltpu.make_async_copy(cot, cbuf, lsem.at[1])
    own_cot.start()
    own_act = pltpu.make_async_copy(act, actx.at[pl.ds(3 + 4 * xh, 4)], lsem.at[0])
    own_act.start()
    wq[:, LANE:] = jnp.zeros((16, LANE), BF)
    wq[:, 0:proj.shape[1]] = proj[...]
    ws1[2 * own] = wq[...]
    pl.semaphore_wait(barrier, len(peers))

    w1 = recvs.take(2 * ny)
    w1_cp = []
    for p in range(ny):
        for sub in range(2):
            if p != own or sub:
                w1_cp.append(
                    send(wq, ws1.at[2 * p + sub], w1 + 2 * p + sub, xlp_s if sub else s, row(yat(-off[p]), xh))
                )

    halo_y = yat(2 * xh - 1)
    nexts, befores = (xlp_s, row(y, xh_p)), (xlp_s, row(y, 1 - xh_p))
    relay_id = recvs.take(4)
    pair_p = send(act.at[pl.ds(0, 2)], qa_p, relay_id, *nexts)
    pair_m = send(act.at[pl.ds(2, 2)], qa_m, relay_id + 1, *befores)
    halo_p = send(act.at[pl.ds(xh, 2)], qh_p, relay_id + 2, *nexts)
    halo_m = send(act.at[pl.ds(xh + 2, 1)], qh_m, relay_id + 3, *befores)
    direct = send(act.at[pl.ds(xh, 3)], actx.at[pl.ds(11 * (1 - xh), 3)], recvs.take(), s, row(halo_y, xh))
    act_cp = [direct]

    def relay_pairs():
        pair_p.wait_recv()
        at = 3 + 4 * (1 - xh_p)
        act_cp.append(send(qa_p, actx.at[pl.ds(at, 2)], recvs.take(), *nexts))
        pair_m.wait_recv()
        at = 5 + 4 * xh_p
        act_cp.append(send(qa_m, actx.at[pl.ds(at, 2)], recvs.take(), *befores))

    def relay_halos():
        halo_p.wait_recv()
        to = row(yat(1 - 2 * xh_p), xh_p)
        act_cp.append(send(qh_p, actx.at[pl.ds(11 * xh_p, 2)], recvs.take(), xlp_s, to))
        halo_m.wait_recv()
        to = row(yat(2 * xh_p - 1), 1 - xh_p)
        act_cp.append(send(qh_m, actx.at[pl.ds(11 * (1 - xh_p) + 2, 1)], recvs.take(), xlp_s, to))

    tf[pl.ds(0, 49), :] = taps[...].astype(F32)
    xp[...] = jnp.zeros_like(xp)
    gain[...] = gain_in[...].reshape(1, chans)
    shift[...] = shift_in[...].reshape(1, chans)
    height, wid = h_ref[0], w_ref[0]
    own_cot.wait()
    cols3 = lax.broadcasted_iota(jnp.int32, (8, width, LANE), 1)
    rows3 = lax.broadcasted_iota(jnp.int32, (8, width, LANE), 0)
    low = lax.broadcasted_iota(jnp.int32, (half_px, LANE), 1) < LANE // 2

    def pack(i, carry):
        lines = pl.ds(pl.multiple_of(i * 8, 8), 8)
        ok = (cols3 < wid) & (rows3 + i * 8 < height)
        main = jnp.where(ok, cbuf[lines, :, 0:LANE].astype(F32), 0.0)
        g_a[i] = main.astype(BF).reshape(2 * half_px, LANE)
        tail = cbuf[lines, :, LANE:].astype(F32)
        tail = jnp.concatenate([tail, tail], axis=-1)
        tail = jnp.where(ok, tail, 0.0).reshape(2 * half_px, LANE)
        g_b[i] = jnp.where(low, tail[:half_px], tail[half_px:]).astype(BF)
        return carry

    lax.fori_loop(0, ny, pack, 0)

    wp_id, wm_id, wc_id = recvs.take(2 * plus), recvs.take(2 * minus), recvs.take(2 * nz)
    wc_cp = []
    wp_cp, wm_cp = {}, {}

    def wblock(sub, z_):
        return wall.at[sec(1 - xl if sub else xl, z_, core)]

    def to_core(sub, z_):
        blk = wblock(sub, z_)
        wc_cp.append(send(blk, blk, wc_id + len(wc_cp), core_s, r))

    def ring_w(t, sub):
        if t < plus:
            blk = wblock(sub, zat(-t))
            wp_cp[t, sub] = send(blk, blk, wp_id + 2 * t + sub, zp_s, r)
        if t < minus:
            blk = wblock(sub, zat(t))
            wm_cp[t, sub] = send(blk, blk, wm_id + 2 * t + sub, zm_s, r)

    low16 = lax.broadcasted_iota(jnp.int32, (16, LANE), 1) < LANE // 2

    def ring_w_open():
        for cp in w1_cp:
            cp.wait_recv()
        for sub in range(2):
            at = sec(1 - xl if sub else xl, z, core)
            for p in range(ny):
                wall[at, :, lanes_of(main_block(p))] = ws1[2 * p + sub, :, 0:LANE]
            for p in range(0, ny, 2):
                first = ws1[2 * p + sub, :, LANE:].astype(F32)
                second = ws1[2 * p + 2 + sub, :, LANE:].astype(F32)
                wall[at, :, lanes_of(pair_block(p))] = jnp.where(
                    low16, first, pltpu.roll(second, LANE // 2, 1)
                ).astype(BF)
        for sub in range(2):
            ring_w(0, sub)
        for sub in range(2):
            to_core(sub, z)

    def ring_w_part(t, sub):
        if t <= plus:
            wp_cp[t - 1, sub].wait_recv()
        wm_cp[t - 1, sub].wait_recv()
        ring_w(t, sub)
        if t <= plus:
            to_core(sub, zat(-t))
        to_core(sub, zat(t))

    def ring_w_step(t):
        ring_w_part(t, 0)
        ring_w_part(t, 1)

    col_ids = lax.broadcasted_iota(jnp.int32, (width, chans), 0)

    def conv(rows_out, flip, lane, put):
        lanes = pl.ds(pl.multiple_of(lane * LANE, LANE), LANE)
        total = [None] * rows_out
        for along in range(7):
            taps_here = []
            for across in range(7):
                i = across * 7 + along
                taps_here.append(tf[pl.ds(48 - i if flip else i, 1), lanes])
            for rho in range(rows_out + 6):
                x = xp[rho, 5 + along:5 + along + width, lanes]
                for out in range(max(0, rho - 6), min(rows_out, rho + 1)):
                    term = taps_here[rho - out] * x
                    total[out] = term if total[out] is None else total[out] + term
        for out in range(rows_out):
            put(out, lanes, total[out])

    relay_pairs()
    ring_w_open()
    relay_halos()

    ring_w_step(1)

    ga_id, gb_id = recvs.take(ny), recvs.take(ny)
    g_cp = {}
    for p in range(ny):
        if p == own:
            continue
        to = yat(-off[p])
        g_cp[p] = (
            send(g_a.at[to], gm.at[main_block(p)], ga_id + p, s, row(to, xh)),
            send(g_b.at[to], gb.at[p], gb_id + p, s, row(to, xh)),
        )
    own_ga = pltpu.make_async_copy(g_a.at[y], gm.at[main_block(own)], lsem.at[1])
    own_gb = pltpu.make_async_copy(g_b.at[y], gb.at[own], lsem.at[2])
    own_ga.start()
    own_gb.start()

    for cp in act_cp:
        cp.wait_recv()
    own_act.wait()

    def expand(i, carry):
        line = 8 * y - 3 + i
        ok = (col_ids < wid) & (line >= 0) & (line < height)
        xp[i, 8:8 + width, :] = jnp.where(ok, actx[i].astype(F32), 0.0)
        return carry

    lax.fori_loop(0, 14, expand, 0)

    def put_mixed(out, lanes, value):
        mx[pl.ds(out * width, width), lanes] = value

    def conv_fwd(lane, carry):
        conv(8, False, lane, put_mixed)
        return carry

    lax.fori_loop(0, chunks // 2, conv_fwd, 0)
    ring_w_step(2)
    lax.fori_loop(chunks // 2, chunks, conv_fwd, 0)

    def norm(i, carry):
        px = pl.ds(pl.multiple_of(i * width, width), width)
        x = mx[px, :]
        centre = jnp.mean(x, axis=-1, keepdims=True)
        dev = x - centre
        inv_spread = 1.0 / jnp.sqrt(jnp.mean(dev * dev, axis=-1, keepdims=True) + EPS)
        unit = dev * inv_spread
        mx[px, :] = unit
        inv[px, :] = jnp.broadcast_to(inv_spread, (width, LANE))
        nrm[px, :] = (unit * gain[...] + shift[...]).astype(BF)
        return carry

    lax.fori_loop(0, 8, norm, 0)
    ring_w_step(3)

    r1_id = recvs.take(2 * nz)
    r1_cp = {}
    order_z = [d for t in range(minus) for d in ((t - minus, plus - t) if t < plus else (t - minus,))] + [0]

    def weight_half(h):
        for p in range(h * quarter, (h + 1) * quarter):
            if p != own:
                g_cp[p][0].wait_recv()
                g_cp[p][1].wait_recv()
            else:
                own_ga.wait()
                own_gb.wait()
        for p in range(h * quarter, (h + 1) * quarter, 2):
            first, second = gb[p].astype(F32), gb[p + 1].astype(F32)
            at = pair_block(p)
            gm[at, 0:half_px, :] = jnp.where(low, first, pltpu.roll(second, LANE // 2, 1)).astype(BF)
            gm[at, half_px:, :] = jnp.where(low, pltpu.roll(first, LANE // 2, 1), second).astype(BF)

        def weight_part(j, carry):
            at = h * per_half + 2 * j
            g2 = jnp.concatenate([gm[at], gm[at + 1]], axis=1)
            lanes = pl.ds(pl.multiple_of(j * 2 * LANE, 2 * LANE), 2 * LANE)
            for i in range(chans // 256):
                part = lax.dot_general(
                    nrm[:, i * 256:(i + 1) * 256], g2, (((0,), (0,)), ((), ())), preferred_element_type=F32
                )
                for q in range(2):
                    xl_, z_ = divmod(8 * i + 4 * q, nz)
                    piece = part[128 * q:128 * q + 128].astype(BF).reshape(4, 2, 16, 2 * LANE)
                    wgp[h, xl_, z_:z_ + 4, :, :, lanes] = piece
            return carry

        lax.fori_loop(0, per_half // 2, weight_part, 0)
        for d in order_z:
            at = zat(d)
            r1_cp[h, d] = send(wgp.at[h, :, at, 1 - core], r1.at[h, :, at], r1_id + h * nz + d + minus, core_s, r)

    rp_id, rm_id = recvs.take(2 * plus), recvs.take(2 * minus)
    rp_cp, rm_cp = {}, {}

    def local_sum(h, xl_, z_):
        return wgp[h, xl_, z_, core].astype(F32) + r1[h, xl_, z_].astype(F32)

    def ring_r(t, h):
        if t < minus:
            r1_cp[h, t - minus].wait_recv()
            if t > 0:
                rm_cp[t - 1, h].wait_recv()
            for xl_ in range(2):
                value = local_sum(h, xl_, zat(t - minus))
                if t > 0:
                    value = value + rm[t - 1, h, xl_].astype(F32)
                sm[t, h, xl_] = value.astype(BF)
            rm_cp[t, h] = send(sm.at[t, h], rm.at[t, h], rm_id + 2 * t + h, zm_s, r)
        if t < plus:
            r1_cp[h, plus - t].wait_recv()
            if t > 0:
                rp_cp[t - 1, h].wait_recv()
            for xl_ in range(2):
                value = local_sum(h, xl_, zat(plus - t))
                if t > 0:
                    value = value + rp[t - 1, h, xl_].astype(F32)
                sp[t, h, xl_] = value.astype(BF)
            rp_cp[t, h] = send(sp.at[t, h], rp.at[t, h], rp_id + 2 * t + h, zp_s, r)

    r4_id = recvs.take(4 * ny)
    r4_cp = []

    def finish(h):
        r1_cp[h, 0].wait_recv()
        rm_cp[minus - 1, h].wait_recv()
        rp_cp[plus - 1, h].wait_recv()
        for sub in range(2):
            xl_ = 1 - xl if sub else xl
            done = local_sum(h, xl_, z) + rm[minus - 1, h, xl_].astype(F32) + rp[plus - 1, h, xl_].astype(F32)
            for p in range(h * quarter, (h + 1) * quarter):
                f4[2 * p + sub, 0] = done[:, lanes_of(main_block(p) - h * per_half)]
                f4[2 * p + sub, 1] = done[:, lanes_of(pair_block(p) - h * per_half)]
        for p in range(h * quarter, (h + 1) * quarter):
            for sub in range(2):
                if p != own or sub:
                    at = 2 * p + sub
                    r4_cp.append(
                        send(f4.at[at], r4.at[at], r4_id + at, xlp_s if sub else s, row(yat(off[p]), xh))
                    )

    gn_id = recvs.take(4 * (chans // 256))
    gn_first, gn_cp = [], []
    mid = gm.shape[1] // 2

    def grad_part(i):
        value = jnp.zeros((gm.shape[1], 256), F32)
        for j in range(blocks // 2):
            g2 = jnp.concatenate([gm[2 * j], gm[2 * j + 1]], axis=1)
            here = wall[16 * i:16 * i + 16, :, lanes_of(2 * j, 2)].reshape(256, 256)
            value = value + lax.dot_general(
                g2, here, (((1,), (1,)), ((), ())), preferred_element_type=F32
            )
        gnp[:, 256 * i:256 * i + 256] = value
        gns[i] = value.astype(BF)
        gn_first.append(send(gns.at[i, pl.ds(0, mid)], qg_p.at[i], gn_id + 4 * i, *nexts))
        gn_first.append(send(gns.at[i, pl.ds(mid, mid)], qg_m.at[i], gn_id + 4 * i + 1, *befores))

    def relay_grad(i):
        gn_first[2 * i].wait_recv()
        gn_cp.append(send(qg_p.at[i], gnr.at[i, pl.ds(0, mid)], gn_id + 4 * i + 2, *nexts))
        gn_first[2 * i + 1].wait_recv()
        gn_cp.append(send(qg_m.at[i], gnr.at[i, pl.ds(mid, mid)], gn_id + 4 * i + 3, *befores))

    def norm_back(i, carry):
        px = pl.ds(pl.multiple_of(i * width, width), width)
        other = jnp.concatenate([gnr[j, px, :] for j in range(chans // 256)], axis=1)
        scaled = (gnp[px, :] + other.astype(F32)) * gain[...]
        unit = mx[px, :]
        first = jnp.mean(scaled, axis=-1, keepdims=True)
        second = jnp.mean(scaled * unit, axis=-1, keepdims=True)
        gmx[3 + i] = (inv[px, 0:1] * (scaled - first - unit * second)).astype(BF)
        return carry

    def expand_back(i, carry):
        at = 4 * xh + i
        line = 8 * y - 3 + at
        ok = (line >= 0) & (line < height_all) & (col_ids >= 0)
        xp[i, 8:8 + width, :] = jnp.where(ok, gmx[at].astype(F32), 0.0)
        return carry

    out_cols = lax.broadcasted_iota(jnp.int32, (width, LANE), 0)

    def put_out(out, lanes, value):
        ok = (out_cols < wid) & (8 * y + 4 * xh + out < height)
        ig[out, :, lanes] = jnp.where(ok, value, 0.0).astype(BF)

    def conv_back(lane, carry):
        conv(4, True, lane, put_out)
        return carry

    weight_half(0)
    ring_r(0, 0)
    ring_w_step(4)
    ring_r(1, 0)
    weight_half(1)
    ring_w_step(5)
    ring_r(0, 1)
    ring_r(2, 0)
    ring_w_step(6)
    ring_r(1, 1)
    for cp in wc_cp:
        cp.wait_recv()
    for i in range(chans // 256):
        grad_part(i)
    ring_r(3, 0)
    ring_r(2, 1)
    for i in range(chans // 256):
        relay_grad(i)
    ring_r(4, 0)
    ring_r(3, 1)
    ring_r(5, 0)
    ring_r(4, 1)
    for cp in gn_cp:
        cp.wait_recv()
    lax.fori_loop(0, 8, norm_back, 0)
    hb_id = recvs.take()
    hb_cp = send(
        gmx.at[pl.ds(8 - 5 * xh, 3)], gmx.at[pl.ds(11 * xh, 3)], hb_id, s, row(yat(1 - 2 * xh), xh)
    )
    finish(0)
    ring_r(5, 1)
    finish(1)
    hb_cp.wait_recv()
    lax.fori_loop(0, 10, expand_back, 0)
    lax.fori_loop(0, chunks, conv_back, 0)
    for cp in r4_cp:
        cp.wait_recv()
    r4[2 * own] = f4[2 * own]
    main, tails = None, [None, None]
    for at in range(2 * ny):
        main = r4[at, 0] if main is None else main + r4[at, 0]
        odd = (at // 2) % 2
        tails[odd] = r4[at, 1] if tails[odd] is None else tails[odd] + r4[at, 1]
    tail = tails[0] + pltpu.roll(tails[1], LANE // 2, 1)
    wg[:, 0:LANE] = main / images
    wg[:, LANE:] = tail[:, 0:LANE // 2] / images

    for cp in started:
        cp.wait_send()
    assert slots.count <= ssem.shape[0] and recvs.count <= rsem.shape[0]


def local(ny, nz, images, activations, cotangent, proj_weight, kernel_taps, ln_gain, ln_shift, heights, widths):
    rows_dev, width, chans = activations.shape[1:]
    height_all, hidden = cotangent.shape[1], cotangent.shape[3]
    blocks = ny + ny // 2
    px = 2 * rows_dev * width
    plus, minus = (nz - 1) // 2, nz // 2
    cols = blocks * LANE
    vmem = pltpu.VMEM
    out = pl.pallas_call(
        functools.partial(kernel_body, ny, nz, float(images)),
        out_shape=(
            pltpu.VMEM((rows_dev, width, chans), BF),
            pltpu.VMEM((16, hidden), F32),
        ),
        in_specs=[pl.BlockSpec(memory_space=pltpu.SMEM)] * 2
        + [pl.BlockSpec(memory_space=pl.ANY)] * 2
        + [pl.BlockSpec(memory_space=vmem)] * 4,
        out_specs=[pl.BlockSpec(memory_space=vmem)] * 2,
        scratch_shapes=[
            vmem((14, width, chans), BF),
            vmem((14, width + 16, chans), F32),
            vmem((56, chans), F32),
            vmem((px, chans), F32),
            vmem((px, LANE), F32),
            vmem((px, chans), BF),
            vmem((height_all, width, hidden), BF),
            vmem((ny, px, LANE), BF),
            vmem((ny, px // 2, LANE), BF),
            vmem((blocks, px, LANE), BF),
            vmem((ny, px // 2, LANE), BF),
            vmem((16, 2 * LANE), BF),
            vmem((2 * ny, 16, 2 * LANE), BF),
            vmem((4 * nz, 16, cols), BF),
            vmem((2, 2, nz, 2, 16, cols // 2), BF),
            vmem((2, 2, nz, 16, cols // 2), BF),
            vmem((plus, 2, 2, 16, cols // 2), BF),
            vmem((minus, 2, 2, 16, cols // 2), BF),
            vmem((plus, 2, 2, 16, cols // 2), BF),
            vmem((minus, 2, 2, 16, cols // 2), BF),
            vmem((2 * ny, 2, 16, LANE), F32),
            vmem((2 * ny, 2, 16, LANE), F32),
            vmem((px, chans), F32),
            vmem((chans // 256, px, 256), BF),
            vmem((chans // 256, px, 256), BF),
            vmem((14, width, chans), BF),
            vmem((1, chans), F32),
            vmem((1, chans), F32),
            vmem((2, width, chans), BF),
            vmem((2, width, chans), BF),
            vmem((2, width, chans), BF),
            vmem((1, width, chans), BF),
            vmem((chans // 256, px // 2, 256), BF),
            vmem((chans // 256, px // 2, 256), BF),
            pltpu.SemaphoreType.DMA((224,)),
            pltpu.SemaphoreType.DMA((224,)),
            pltpu.SemaphoreType.DMA((3,)),
        ],
        compiler_params=pltpu.CompilerParams(
            collective_id=0, has_side_effects=True, vmem_limit_bytes=60 * 1024 * 1024
        ),
    )(
        heights, widths, activations[0], cotangent[0], proj_weight, kernel_taps,
        ln_gain, ln_shift,
    )
    return out[0][None], out[1]


def solution(mesh):
    ny = mesh.shape["rows"] // 2
    nz = mesh.shape["section"] // 4
    in_specs = (
        P("section", "rows", None, None),
        P("section", None, None, "rows"),
        P("section", "rows"),
        P(),
        P(),
        P(),
        P("section"),
        P("section"),
    )
    out_specs = (P("section", "rows", None, None), P("section", "rows"))
    body = functools.partial(local, ny, nz, mesh.shape["section"])
    return jax.shard_map(body, mesh=mesh, in_specs=in_specs, out_specs=out_specs, check_vma=False)
```

```python
import functools

import jax
import jax.numpy as jnp
from jax import lax
from jax.experimental import pallas as pl
from jax.experimental.pallas import tpu as pltpu
from jax.sharding import PartitionSpec as P

EPS = 1e-06
BF = jnp.bfloat16
F32 = jnp.float32
LANE = 128


class Slots:
    def __init__(self):
        self.count = 0

    def take(self, n=1):
        first = self.count
        self.count += n
        return first


def kernel_body(
    ny, nz, images,
    h_ref, w_ref, act, cot, proj, taps, gain_in, shift_in,
    ig, wg,
    actx, xp, tf, mx, inv, nrm, cbuf, g_a, g_b, gm, gb, wq, ws1, wall, wgp, r1, sp, sm, rp, rm,
    f4, r4, gnp, gns, gnr, gmx, gain, shift, qa_p, qa_m, qh_p, qh_m, qg_p, qg_m, ssem, rsem, lsem,
):
    s = lax.axis_index("section")
    r = lax.axis_index("rows")
    core = lax.rem(s, 2)
    z = lax.rem(lax.div(s, 2), nz)
    xl = lax.div(s, 2 * nz)
    y = lax.div(r, 2)
    xh = lax.rem(r, 2)
    width, chans = act.shape[1], act.shape[2]
    chunks = chans // LANE
    height_all = cot.shape[0]
    half_px = g_b.shape[1]
    plus, minus = (nz - 1) // 2, nz // 2
    quarter = ny // 2
    per_half = quarter + quarter // 2
    blocks = 2 * per_half
    off = sorted(range(ny), key=lambda k: min(k, ny - k))
    own = off.index(0)

    def main_block(p):
        return per_half * (p // quarter) + p % quarter

    def pair_block(p):
        return per_half * (p // quarter) + quarter + (p % quarter) // 2

    def sec(xl_, z_, c_):
        return (xl_ * nz + z_) * 2 + c_

    def yat(k):
        return lax.rem(y + k + ny, ny)

    def zat(k):
        return lax.rem(z + k + 2 * nz, nz)

    def row(y_, xh_):
        return y_ * 2 + xh_

    def lanes_of(i, n=1):
        return slice(i * LANE, (i + n) * LANE)

    slots = Slots()
    recvs = Slots()
    started = []

    def send(src, dst, recv, s_, r_):
        cp = pltpu.make_async_remote_copy(
            src_ref=src, dst_ref=dst, send_sem=ssem.at[slots.take()], recv_sem=rsem.at[recv],
            device_id={"section": s_, "rows": r_}, device_id_type=pl.DeviceIdType.MESH,
        )
        cp.start()
        started.append(cp)
        return cp

    core_s = sec(xl, z, 1 - core)
    xlp_s = sec(1 - xl, z, core)
    xh_p = lax.rem(xh + xl, 2)
    zp_s = sec(xl, zat(1), core)
    zm_s = sec(xl, zat(-1), core)

    barrier = pltpu.get_barrier_semaphore()
    peers = [(xs, row(yat(k), xh)) for k in range(ny) for xs in (s, xlp_s) if not (k == 0 and xs is s)]
    peers += [(xlp_s, row(yat(k), 1 - xh)) for k in (0, 1, -1)]
    peers += [(core_s, r), (zp_s, r), (zm_s, r)]
    for s_, r_ in peers:
        pl.semaphore_signal(
            barrier, inc=1, device_id={"section": s_, "rows": r_},
            device_id_type=pl.DeviceIdType.MESH,
        )

    own_cot = pltpu.make_async_copy(cot, cbuf, lsem.at[1])
    own_cot.start()
    own_act = pltpu.make_async_copy(act, actx.at[pl.ds(3 + 4 * xh, 4)], lsem.at[0])
    own_act.start()
    wq[:, LANE:] = jnp.zeros((16, LANE), BF)
    wq[:, 0:proj.shape[1]] = proj[...]
    ws1[2 * own] = wq[...]
    pl.semaphore_wait(barrier, len(peers))

    w1 = recvs.take(2 * ny)
    w1_cp = []
    for p in range(ny):
        for sub in range(2):
            if p != own or sub:
                w1_cp.append(
                    send(wq, ws1.at[2 * p + sub], w1 + 2 * p + sub, xlp_s if sub else s, row(yat(-off[p]), xh))
                )

    halo_y = yat(2 * xh - 1)
    nexts, befores = (xlp_s, row(y, xh_p)), (xlp_s, row(y, 1 - xh_p))
    relay_id = recvs.take(4)
    pair_p = send(act.at[pl.ds(0, 2)], qa_p, relay_id, *nexts)
    pair_m = send(act.at[pl.ds(2, 2)], qa_m, relay_id + 1, *befores)
    halo_p = send(act.at[pl.ds(xh, 2)], qh_p, relay_id + 2, *nexts)
    halo_m = send(act.at[pl.ds(xh + 2, 1)], qh_m, relay_id + 3, *befores)
    direct = send(act.at[pl.ds(xh, 3)], actx.at[pl.ds(11 * (1 - xh), 3)], recvs.take(), s, row(halo_y, xh))
    act_cp = [direct]

    def relay_pairs():
        pair_p.wait_recv()
        at = 3 + 4 * (1 - xh_p)
        act_cp.append(send(qa_p, actx.at[pl.ds(at, 2)], recvs.take(), *nexts))
        pair_m.wait_recv()
        at = 5 + 4 * xh_p
        act_cp.append(send(qa_m, actx.at[pl.ds(at, 2)], recvs.take(), *befores))

    def relay_halos():
        halo_p.wait_recv()
        to = row(yat(1 - 2 * xh_p), xh_p)
        act_cp.append(send(qh_p, actx.at[pl.ds(11 * xh_p, 2)], recvs.take(), xlp_s, to))
        halo_m.wait_recv()
        to = row(yat(2 * xh_p - 1), 1 - xh_p)
        act_cp.append(send(qh_m, actx.at[pl.ds(11 * (1 - xh_p) + 2, 1)], recvs.take(), xlp_s, to))

    tf[pl.ds(0, 49), :] = taps[...].astype(F32)
    xp[...] = jnp.zeros_like(xp)
    gain[...] = gain_in[...].reshape(1, chans)
    shift[...] = shift_in[...].reshape(1, chans)
    height, wid = h_ref[0], w_ref[0]
    own_cot.wait()
    cols3 = lax.broadcasted_iota(jnp.int32, (8, width, LANE), 1)
    rows3 = lax.broadcasted_iota(jnp.int32, (8, width, LANE), 0)
    low = lax.broadcasted_iota(jnp.int32, (half_px, LANE), 1) < LANE // 2

    def pack(i, carry):
        lines = pl.ds(pl.multiple_of(i * 8, 8), 8)
        ok = (cols3 < wid) & (rows3 + i * 8 < height)
        main = jnp.where(ok, cbuf[lines, :, 0:LANE].astype(F32), 0.0)
        g_a[i] = main.astype(BF).reshape(2 * half_px, LANE)
        tail = cbuf[lines, :, LANE:].astype(F32)
        tail = jnp.concatenate([tail, tail], axis=-1)
        tail = jnp.where(ok, tail, 0.0).reshape(2 * half_px, LANE)
        g_b[i] = jnp.where(low, tail[:half_px], tail[half_px:]).astype(BF)
        return carry

    lax.fori_loop(0, ny, pack, 0)

    wp_id, wm_id, wc_id = recvs.take(2 * plus), recvs.take(2 * minus), recvs.take(2 * nz)
    wc_cp = []
    wp_cp, wm_cp = {}, {}

    def wblock(sub, z_):
        return wall.at[sec(1 - xl if sub else xl, z_, core)]

    def to_core(sub, z_):
        blk = wblock(sub, z_)
        wc_cp.append(send(blk, blk, wc_id + len(wc_cp), core_s, r))

    def ring_w(t, sub):
        if t < plus:
            blk = wblock(sub, zat(-t))
            wp_cp[t, sub] = send(blk, blk, wp_id + 2 * t + sub, zp_s, r)
        if t < minus:
            blk = wblock(sub, zat(t))
            wm_cp[t, sub] = send(blk, blk, wm_id + 2 * t + sub, zm_s, r)

    low16 = lax.broadcasted_iota(jnp.int32, (16, LANE), 1) < LANE // 2

    def ring_w_open():
        for cp in w1_cp:
            cp.wait_recv()
        for sub in range(2):
            at = sec(1 - xl if sub else xl, z, core)
            for p in range(ny):
                wall[at, :, lanes_of(main_block(p))] = ws1[2 * p + sub, :, 0:LANE]
            for p in range(0, ny, 2):
                first = ws1[2 * p + sub, :, LANE:].astype(F32)
                second = ws1[2 * p + 2 + sub, :, LANE:].astype(F32)
                wall[at, :, lanes_of(pair_block(p))] = jnp.where(
                    low16, first, pltpu.roll(second, LANE // 2, 1)
                ).astype(BF)
        for sub in range(2):
            ring_w(0, sub)
        for sub in range(2):
            to_core(sub, z)

    def ring_w_part(t, sub):
        if t <= plus:
            wp_cp[t - 1, sub].wait_recv()
        wm_cp[t - 1, sub].wait_recv()
        ring_w(t, sub)
        if t <= plus:
            to_core(sub, zat(-t))
        to_core(sub, zat(t))

    def ring_w_step(t):
        ring_w_part(t, 0)
        ring_w_part(t, 1)

    col_ids = lax.broadcasted_iota(jnp.int32, (width, chans), 0)

    def conv(rows_out, flip, lane, put):
        lanes = pl.ds(pl.multiple_of(lane * LANE, LANE), LANE)
        total = [None] * rows_out
        for along in range(7):
            taps_here = []
            for across in range(7):
                i = across * 7 + along
                taps_here.append(tf[pl.ds(48 - i if flip else i, 1), lanes])
            for rho in range(rows_out + 6):
                x = xp[rho, 5 + along:5 + along + width, lanes]
                for out in range(max(0, rho - 6), min(rows_out, rho + 1)):
                    term = taps_here[rho - out] * x
                    total[out] = term if total[out] is None else total[out] + term
        for out in range(rows_out):
            put(out, lanes, total[out])

    relay_pairs()
    ring_w_open()
    relay_halos()

    ga_id, gb_id = recvs.take(ny), recvs.take(ny)
    g_cp = {}

    def send_half(h):
        for p in range(h * quarter, (h + 1) * quarter):
            if p == own:
                continue
            to = yat(-off[p])
            g_cp[p] = (
                send(g_a.at[to], gm.at[main_block(p)], ga_id + p, s, row(to, xh)),
                send(g_b.at[to], gb.at[p], gb_id + p, s, row(to, xh)),
            )

    send_half(0)
    own_ga = pltpu.make_async_copy(g_a.at[y], gm.at[main_block(own)], lsem.at[1])
    own_gb = pltpu.make_async_copy(g_b.at[y], gb.at[own], lsem.at[2])
    own_ga.start()
    own_gb.start()
    ring_w_step(1)
    send_half(1)

    for cp in act_cp:
        cp.wait_recv()
    own_act.wait()

    def expand(i, carry):
        line = 8 * y - 3 + i
        ok = (col_ids < wid) & (line >= 0) & (line < height)
        xp[i, 8:8 + width, :] = jnp.where(ok, actx[i].astype(F32), 0.0)
        return carry

    lax.fori_loop(0, 14, expand, 0)

    def put_mixed(out, lanes, value):
        mx[pl.ds(out * width, width), lanes] = value

    def conv_fwd(lane, carry):
        conv(8, False, lane, put_mixed)
        return carry

    lax.fori_loop(0, chunks // 2, conv_fwd, 0)
    ring_w_step(2)
    lax.fori_loop(chunks // 2, chunks, conv_fwd, 0)

    def norm(i, carry):
        px = pl.ds(pl.multiple_of(i * width, width), width)
        x = mx[px, :]
        centre = jnp.mean(x, axis=-1, keepdims=True)
        dev = x - centre
        inv_spread = 1.0 / jnp.sqrt(jnp.mean(dev * dev, axis=-1, keepdims=True) + EPS)
        unit = dev * inv_spread
        mx[px, :] = unit
        inv[px, :] = jnp.broadcast_to(inv_spread, (width, LANE))
        nrm[px, :] = (unit * gain[...] + shift[...]).astype(BF)
        return carry

    lax.fori_loop(0, 8, norm, 0)
    ring_w_step(3)

    r1_id = recvs.take(2 * nz)
    r1_cp = {}
    order_z = [d for t in range(minus) for d in ((t - minus, plus - t) if t < plus else (t - minus,))] + [0]

    def weight_half(h):
        for p in range(h * quarter, (h + 1) * quarter):
            if p != own:
                g_cp[p][0].wait_recv()
                g_cp[p][1].wait_recv()
            else:
                own_ga.wait()
                own_gb.wait()
        for p in range(h * quarter, (h + 1) * quarter, 2):
            first, second = gb[p].astype(F32), gb[p + 1].astype(F32)
            at = pair_block(p)
            gm[at, 0:half_px, :] = jnp.where(low, first, pltpu.roll(second, LANE // 2, 1)).astype(BF)
            gm[at, half_px:, :] = jnp.where(low, pltpu.roll(first, LANE // 2, 1), second).astype(BF)

        def weight_part(j, carry):
            at = h * per_half + 2 * j
            g2 = jnp.concatenate([gm[at], gm[at + 1]], axis=1)
            lanes = pl.ds(pl.multiple_of(j * 2 * LANE, 2 * LANE), 2 * LANE)
            for i in range(chans // 256):
                part = lax.dot_general(
                    nrm[:, i * 256:(i + 1) * 256], g2, (((0,), (0,)), ((), ())), preferred_element_type=F32
                )
                for q in range(2):
                    xl_, z_ = divmod(8 * i + 4 * q, nz)
                    piece = part[128 * q:128 * q + 128].astype(BF).reshape(4, 2, 16, 2 * LANE)
                    wgp[h, xl_, z_:z_ + 4, :, :, lanes] = piece
            return carry

        lax.fori_loop(0, per_half // 2, weight_part, 0)
        for d in order_z:
            at = zat(d)
            r1_cp[h, d] = send(wgp.at[h, :, at, 1 - core], r1.at[h, :, at], r1_id + h * nz + d + minus, core_s, r)

    rp_id, rm_id = recvs.take(2 * plus), recvs.take(2 * minus)
    rp_cp, rm_cp = {}, {}

    def local_sum(h, xl_, z_):
        return wgp[h, xl_, z_, core].astype(F32) + r1[h, xl_, z_].astype(F32)

    def ring_r(t, h):
        if t < minus:
            r1_cp[h, t - minus].wait_recv()
            if t > 0:
                rm_cp[t - 1, h].wait_recv()
            for xl_ in range(2):
                value = local_sum(h, xl_, zat(t - minus))
                if t > 0:
                    value = value + rm[t - 1, h, xl_].astype(F32)
                sm[t, h, xl_] = value.astype(BF)
            rm_cp[t, h] = send(sm.at[t, h], rm.at[t, h], rm_id + 2 * t + h, zm_s, r)
        if t < plus:
            r1_cp[h, plus - t].wait_recv()
            if t > 0:
                rp_cp[t - 1, h].wait_recv()
            for xl_ in range(2):
                value = local_sum(h, xl_, zat(plus - t))
                if t > 0:
                    value = value + rp[t - 1, h, xl_].astype(F32)
                sp[t, h, xl_] = value.astype(BF)
            rp_cp[t, h] = send(sp.at[t, h], rp.at[t, h], rp_id + 2 * t + h, zp_s, r)

    r4_id = recvs.take(4 * ny)
    r4_cp = []

    def finish(h):
        r1_cp[h, 0].wait_recv()
        rm_cp[minus - 1, h].wait_recv()
        rp_cp[plus - 1, h].wait_recv()
        for sub in range(2):
            xl_ = 1 - xl if sub else xl
            done = local_sum(h, xl_, z) + rm[minus - 1, h, xl_].astype(F32) + rp[plus - 1, h, xl_].astype(F32)
            for p in range(h * quarter, (h + 1) * quarter):
                f4[2 * p + sub, 0] = done[:, lanes_of(main_block(p) - h * per_half)]
                f4[2 * p + sub, 1] = done[:, lanes_of(pair_block(p) - h * per_half)]
        for p in range(h * quarter, (h + 1) * quarter):
            for sub in range(2):
                if p != own or sub:
                    at = 2 * p + sub
                    r4_cp.append(
                        send(f4.at[at], r4.at[at], r4_id + at, xlp_s if sub else s, row(yat(off[p]), xh))
                    )

    gn_id = recvs.take(4 * (chans // 256))
    gn_first, gn_cp = [], []
    mid = gm.shape[1] // 2

    def grad_part(i):
        value = jnp.zeros((gm.shape[1], 256), F32)
        for j in range(blocks // 2):
            g2 = jnp.concatenate([gm[2 * j], gm[2 * j + 1]], axis=1)
            here = wall[16 * i:16 * i + 16, :, lanes_of(2 * j, 2)].reshape(256, 256)
            value = value + lax.dot_general(
                g2, here, (((1,), (1,)), ((), ())), preferred_element_type=F32
            )
        gnp[:, 256 * i:256 * i + 256] = value
        gns[i] = value.astype(BF)
        gn_first.append(send(gns.at[i, pl.ds(0, mid)], qg_p.at[i], gn_id + 4 * i, *nexts))
        gn_first.append(send(gns.at[i, pl.ds(mid, mid)], qg_m.at[i], gn_id + 4 * i + 1, *befores))

    def relay_grad(i):
        gn_first[2 * i].wait_recv()
        gn_cp.append(send(qg_p.at[i], gnr.at[i, pl.ds(0, mid)], gn_id + 4 * i + 2, *nexts))
        gn_first[2 * i + 1].wait_recv()
        gn_cp.append(send(qg_m.at[i], gnr.at[i, pl.ds(mid, mid)], gn_id + 4 * i + 3, *befores))

    def norm_back(i, carry):
        px = pl.ds(pl.multiple_of(i * width, width), width)
        other = jnp.concatenate([gnr[j, px, :] for j in range(chans // 256)], axis=1)
        scaled = (gnp[px, :] + other.astype(F32)) * gain[...]
        unit = mx[px, :]
        first = jnp.mean(scaled, axis=-1, keepdims=True)
        second = jnp.mean(scaled * unit, axis=-1, keepdims=True)
        gmx[3 + i] = (inv[px, 0:1] * (scaled - first - unit * second)).astype(BF)
        return carry

    def expand_back(i, carry):
        at = 4 * xh + i
        line = 8 * y - 3 + at
        ok = (line >= 0) & (line < height_all) & (col_ids >= 0)
        xp[i, 8:8 + width, :] = jnp.where(ok, gmx[at].astype(F32), 0.0)
        return carry

    out_cols = lax.broadcasted_iota(jnp.int32, (width, LANE), 0)

    def put_out(out, lanes, value):
        ok = (out_cols < wid) & (8 * y + 4 * xh + out < height)
        ig[out, :, lanes] = jnp.where(ok, value, 0.0).astype(BF)

    def conv_back(lane, carry):
        conv(4, True, lane, put_out)
        return carry

    weight_half(0)
    ring_w_step(4)
    ring_r(0, 0)
    ring_r(1, 0)
    ring_w_step(5)
    weight_half(1)
    ring_r(0, 1)
    ring_r(2, 0)
    ring_w_step(6)
    for cp in wc_cp:
        cp.wait_recv()
    for i in range(chans // 256):
        grad_part(i)
    ring_r(1, 1)
    ring_r(3, 0)
    ring_r(2, 1)
    for i in range(chans // 256):
        relay_grad(i)
    ring_r(4, 0)
    ring_r(3, 1)
    ring_r(5, 0)
    ring_r(4, 1)
    for cp in gn_cp:
        cp.wait_recv()
    lax.fori_loop(0, 8, norm_back, 0)
    hb_id = recvs.take()
    hb_cp = send(
        gmx.at[pl.ds(8 - 5 * xh, 3)], gmx.at[pl.ds(11 * xh, 3)], hb_id, s, row(yat(1 - 2 * xh), xh)
    )
    finish(0)
    ring_r(5, 1)
    finish(1)
    hb_cp.wait_recv()
    lax.fori_loop(0, 10, expand_back, 0)
    lax.fori_loop(0, chunks, conv_back, 0)
    for cp in r4_cp:
        cp.wait_recv()
    r4[2 * own] = f4[2 * own]
    main, tails = None, [None, None]
    for at in range(2 * ny):
        main = r4[at, 0] if main is None else main + r4[at, 0]
        odd = (at // 2) % 2
        tails[odd] = r4[at, 1] if tails[odd] is None else tails[odd] + r4[at, 1]
    tail = tails[0] + pltpu.roll(tails[1], LANE // 2, 1)
    wg[:, 0:LANE] = main / images
    wg[:, LANE:] = tail[:, 0:LANE // 2] / images

    for cp in started:
        cp.wait_send()
    assert slots.count <= ssem.shape[0] and recvs.count <= rsem.shape[0]


def local(ny, nz, images, activations, cotangent, proj_weight, kernel_taps, ln_gain, ln_shift, heights, widths):
    rows_dev, width, chans = activations.shape[1:]
    height_all, hidden = cotangent.shape[1], cotangent.shape[3]
    blocks = ny + ny // 2
    px = 2 * rows_dev * width
    plus, minus = (nz - 1) // 2, nz // 2
    cols = blocks * LANE
    vmem = pltpu.VMEM
    out = pl.pallas_call(
        functools.partial(kernel_body, ny, nz, float(images)),
        out_shape=(
            pltpu.VMEM((rows_dev, width, chans), BF),
            pltpu.VMEM((16, hidden), F32),
        ),
        in_specs=[pl.BlockSpec(memory_space=pltpu.SMEM)] * 2
        + [pl.BlockSpec(memory_space=pl.ANY)] * 2
        + [pl.BlockSpec(memory_space=vmem)] * 4,
        out_specs=[pl.BlockSpec(memory_space=vmem)] * 2,
        scratch_shapes=[
            vmem((14, width, chans), BF),
            vmem((14, width + 16, chans), F32),
            vmem((56, chans), F32),
            vmem((px, chans), F32),
            vmem((px, LANE), F32),
            vmem((px, chans), BF),
            vmem((height_all, width, hidden), BF),
            vmem((ny, px, LANE), BF),
            vmem((ny, px // 2, LANE), BF),
            vmem((blocks, px, LANE), BF),
            vmem((ny, px // 2, LANE), BF),
            vmem((16, 2 * LANE), BF),
            vmem((2 * ny, 16, 2 * LANE), BF),
            vmem((4 * nz, 16, cols), BF),
            vmem((2, 2, nz, 2, 16, cols // 2), BF),
            vmem((2, 2, nz, 16, cols // 2), BF),
            vmem((plus, 2, 2, 16, cols // 2), BF),
            vmem((minus, 2, 2, 16, cols // 2), BF),
            vmem((plus, 2, 2, 16, cols // 2), BF),
            vmem((minus, 2, 2, 16, cols // 2), BF),
            vmem((2 * ny, 2, 16, LANE), F32),
            vmem((2 * ny, 2, 16, LANE), F32),
            vmem((px, chans), F32),
            vmem((chans // 256, px, 256), BF),
            vmem((chans // 256, px, 256), BF),
            vmem((14, width, chans), BF),
            vmem((1, chans), F32),
            vmem((1, chans), F32),
            vmem((2, width, chans), BF),
            vmem((2, width, chans), BF),
            vmem((2, width, chans), BF),
            vmem((1, width, chans), BF),
            vmem((chans // 256, px // 2, 256), BF),
            vmem((chans // 256, px // 2, 256), BF),
            pltpu.SemaphoreType.DMA((224,)),
            pltpu.SemaphoreType.DMA((224,)),
            pltpu.SemaphoreType.DMA((3,)),
        ],
        compiler_params=pltpu.CompilerParams(
            collective_id=0, has_side_effects=True, vmem_limit_bytes=60 * 1024 * 1024
        ),
    )(
        heights, widths, activations[0], cotangent[0], proj_weight, kernel_taps,
        ln_gain, ln_shift,
    )
    return out[0][None], out[1]


def solution(mesh):
    ny = mesh.shape["rows"] // 2
    nz = mesh.shape["section"] // 4
    in_specs = (
        P("section", "rows", None, None),
        P("section", None, None, "rows"),
        P("section", "rows"),
        P(),
        P(),
        P(),
        P("section"),
        P("section"),
    )
    out_specs = (P("section", "rows", None, None), P("section", "rows"))
    body = functools.partial(local, ny, nz, mesh.shape["section"])
    return jax.shard_map(body, mesh=mesh, in_specs=in_specs, out_specs=out_specs, check_vma=False)
```

```python
import functools

import jax
import jax.numpy as jnp
from jax import lax
from jax.experimental import pallas as pl
from jax.experimental.pallas import tpu as pltpu
from jax.sharding import PartitionSpec as P

EPS = 1e-06
BF = jnp.bfloat16
F32 = jnp.float32
LANE = 128


class Slots:
    def __init__(self):
        self.count = 0

    def take(self, n=1):
        first = self.count
        self.count += n
        return first


def kernel_body(
    ny, nz, images,
    h_ref, w_ref, act, cot, proj, taps, gain_in, shift_in,
    ig, wg,
    actx, xp, tf, mx, inv, nrm, cbuf, g_a, g_b, gm, gb, wq, ws1, wall, wgp, r1, sp, sm, rp, rm,
    f4, r4, gnp, gns, gnr, gmx, gain, shift, ssem, rsem, lsem,
):
    s = lax.axis_index("section")
    r = lax.axis_index("rows")
    core = lax.rem(s, 2)
    z = lax.rem(lax.div(s, 2), nz)
    xl = lax.div(s, 2 * nz)
    y = lax.div(r, 2)
    xh = lax.rem(r, 2)
    width, chans = act.shape[1], act.shape[2]
    chunks = chans // LANE
    height_all = cot.shape[0]
    half_px = g_b.shape[1]
    plus, minus = (nz - 1) // 2, nz // 2
    quarter = ny // 2
    per_half = quarter + quarter // 2
    blocks = 2 * per_half
    off = sorted(range(ny), key=lambda k: min(k, ny - k))

    def main_block(p):
        return per_half * (p // quarter) + p % quarter

    def pair_block(p):
        return per_half * (p // quarter) + quarter + (p % quarter) // 2

    def sec(xl_, z_, c_):
        return (xl_ * nz + z_) * 2 + c_

    def yat(k):
        return lax.rem(y + k + ny, ny)

    def zat(k):
        return lax.rem(z + k + 2 * nz, nz)

    def row(y_, xh_):
        return y_ * 2 + xh_

    def lanes_of(i, n=1):
        return slice(i * LANE, (i + n) * LANE)

    slots = Slots()
    recvs = Slots()
    started = []

    def send(src, dst, recv, s_, r_):
        cp = pltpu.make_async_remote_copy(
            src_ref=src, dst_ref=dst, send_sem=ssem.at[slots.take()], recv_sem=rsem.at[recv],
            device_id={"section": s_, "rows": r_}, device_id_type=pl.DeviceIdType.MESH,
        )
        cp.start()
        started.append(cp)
        return cp

    core_s = sec(xl, z, 1 - core)
    xlp_s = sec(1 - xl, z, core)
    zp_s = sec(xl, zat(1), core)
    zm_s = sec(xl, zat(-1), core)

    barrier = pltpu.get_barrier_semaphore()
    peers = [(xs, row(yat(k), xh)) for k in range(ny) for xs in (s, xlp_s) if not (k == 0 and xs is s)]
    peers += [(s, row(y, 1 - xh)), (s, row(yat(1), 1 - xh)), (s, row(yat(-1), 1 - xh))]
    peers += [(core_s, r), (zp_s, r), (zm_s, r)]
    for s_, r_ in peers:
        pl.semaphore_signal(
            barrier, inc=1, device_id={"section": s_, "rows": r_},
            device_id_type=pl.DeviceIdType.MESH,
        )

    own_cot = pltpu.make_async_copy(cot, cbuf, lsem.at[1])
    own_cot.start()
    own_act = pltpu.make_async_copy(act, actx.at[pl.ds(3 + 4 * xh, 4)], lsem.at[0])
    own_act.start()
    wq[:, LANE:] = jnp.zeros((16, LANE), BF)
    wq[:, 0:proj.shape[1]] = proj[...]
    ws1[0] = wq[...]
    tf[pl.ds(0, 49), :] = taps[...].astype(F32)
    xp[...] = jnp.zeros_like(xp)
    gain[...] = gain_in[...].reshape(1, chans)
    shift[...] = shift_in[...].reshape(1, chans)
    height, wid = h_ref[0], w_ref[0]
    own_cot.wait()
    cols3 = lax.broadcasted_iota(jnp.int32, (8, width, LANE), 1)
    rows3 = lax.broadcasted_iota(jnp.int32, (8, width, LANE), 0)
    low = lax.broadcasted_iota(jnp.int32, (half_px, LANE), 1) < LANE // 2

    def pack(i, carry):
        lines = pl.ds(pl.multiple_of(i * 8, 8), 8)
        ok = (cols3 < wid) & (rows3 + i * 8 < height)
        main = jnp.where(ok, cbuf[lines, :, 0:LANE].astype(F32), 0.0)
        g_a[i] = main.astype(BF).reshape(2 * half_px, LANE)
        tail = cbuf[lines, :, LANE:].astype(F32)
        tail = jnp.concatenate([tail, tail], axis=-1)
        tail = jnp.where(ok, tail, 0.0).reshape(2 * half_px, LANE)
        g_b[i] = jnp.where(low, tail[:half_px], tail[half_px:]).astype(BF)
        return carry

    lax.fori_loop(0, ny, pack, 0)
    pl.semaphore_wait(barrier, len(peers))

    w1 = recvs.take(2 * ny)
    w1_cp = []
    for p in range(ny):
        for sub in range(2):
            if p or sub:
                w1_cp.append(
                    send(wq, ws1.at[2 * p + sub], w1 + 2 * p + sub, xlp_s if sub else s, row(yat(-off[p]), xh))
                )

    a_pair, a_halo = recvs.take(), recvs.take(2)
    pair_cp = send(act, actx.at[pl.ds(3 + 4 * xh, 4)], a_pair, s, row(y, 1 - xh))
    halo_y = yat(2 * xh - 1)
    for to in range(2):
        halo_cp = send(
            act.at[pl.ds(xh, 3)], actx.at[pl.ds(11 * (1 - xh), 3)], a_halo + xh, s, row(halo_y, to)
        )

    wp_id, wm_id, wc_id = recvs.take(2 * plus), recvs.take(2 * minus), recvs.take(2 * nz)
    wc_cp = []
    wp_cp, wm_cp = {}, {}

    def wblock(sub, z_):
        return wall.at[sec(1 - xl if sub else xl, z_, core)]

    def to_core(sub, z_):
        blk = wblock(sub, z_)
        wc_cp.append(send(blk, blk, wc_id + len(wc_cp), core_s, r))

    def ring_w(t, sub):
        if t < plus:
            blk = wblock(sub, zat(-t))
            wp_cp[t, sub] = send(blk, blk, wp_id + 2 * t + sub, zp_s, r)
        if t < minus:
            blk = wblock(sub, zat(t))
            wm_cp[t, sub] = send(blk, blk, wm_id + 2 * t + sub, zm_s, r)

    low16 = lax.broadcasted_iota(jnp.int32, (16, LANE), 1) < LANE // 2

    def ring_w_open():
        for cp in w1_cp:
            cp.wait_recv()
        for sub in range(2):
            at = sec(1 - xl if sub else xl, z, core)
            for p in range(ny):
                wall[at, :, lanes_of(main_block(p))] = ws1[2 * p + sub, :, 0:LANE]
            for p in range(0, ny, 2):
                first = ws1[2 * p + sub, :, LANE:].astype(F32)
                second = ws1[2 * p + 2 + sub, :, LANE:].astype(F32)
                wall[at, :, lanes_of(pair_block(p))] = jnp.where(
                    low16, first, pltpu.roll(second, LANE // 2, 1)
                ).astype(BF)
        for sub in range(2):
            ring_w(0, sub)
        for sub in range(2):
            to_core(sub, z)

    def ring_w_step(t):
        for sub in range(2):
            if t <= plus:
                wp_cp[t - 1, sub].wait_recv()
            wm_cp[t - 1, sub].wait_recv()
            ring_w(t, sub)
            if t <= plus:
                to_core(sub, zat(-t))
            to_core(sub, zat(t))

    col_ids = lax.broadcasted_iota(jnp.int32, (width, chans), 0)

    def conv(rows_out, flip, lane, put):
        lanes = pl.ds(pl.multiple_of(lane * LANE, LANE), LANE)
        total = [None] * rows_out
        for along in range(7):
            taps_here = []
            for across in range(7):
                i = across * 7 + along
                taps_here.append(tf[pl.ds(48 - i if flip else i, 1), lanes])
            for rho in range(rows_out + 6):
                x = xp[rho, 5 + along:5 + along + width, lanes]
                for out in range(max(0, rho - 6), min(rows_out, rho + 1)):
                    term = taps_here[rho - out] * x
                    total[out] = term if total[out] is None else total[out] + term
        for out in range(rows_out):
            put(out, lanes, total[out])

    ring_w_open()

    ga_id, gb_id = recvs.take(ny), recvs.take(ny)
    g_cp = {}
    for p in range(1, ny):
        to = yat(-off[p])
        g_cp[p] = (
            send(g_a.at[to], gm.at[main_block(p)], ga_id + p, s, row(to, xh)),
            send(g_b.at[to], gb.at[p], gb_id + p, s, row(to, xh)),
        )
    own_ga = pltpu.make_async_copy(g_a.at[y], gm.at[0], lsem.at[1])
    own_gb = pltpu.make_async_copy(g_b.at[y], gb.at[0], lsem.at[2])
    own_ga.start()
    own_gb.start()

    ring_w_step(1)
    pair_cp.wait_recv()
    for i in range(2):
        pltpu.make_async_remote_copy(
            src_ref=act.at[pl.ds(xh, 3)], dst_ref=actx.at[pl.ds(11 * (1 - i), 3)],
            send_sem=ssem.at[0], recv_sem=rsem.at[a_halo + i],
            device_id={"section": s, "rows": row(halo_y, 0)}, device_id_type=pl.DeviceIdType.MESH,
        ).wait_recv()
    own_act.wait()

    def expand(i, carry):
        line = 8 * y - 3 + i
        ok = (col_ids < wid) & (line >= 0) & (line < height)
        xp[i, 8:8 + width, :] = jnp.where(ok, actx[i].astype(F32), 0.0)
        return carry

    lax.fori_loop(0, 14, expand, 0)

    def put_mixed(out, lanes, value):
        mx[pl.ds(out * width, width), lanes] = value

    def conv_fwd(lane, carry):
        conv(8, False, lane, put_mixed)
        return carry

    ring_w_step(2)
    lax.fori_loop(0, chunks // 3, conv_fwd, 0)
    ring_w_step(3)
    lax.fori_loop(chunks // 3, 2 * chunks // 3, conv_fwd, 0)
    ring_w_step(4)
    lax.fori_loop(2 * chunks // 3, chunks, conv_fwd, 0)
    ring_w_step(5)

    def norm(i, carry):
        px = pl.ds(pl.multiple_of(i * width, width), width)
        x = mx[px, :]
        centre = jnp.mean(x, axis=-1, keepdims=True)
        dev = x - centre
        inv_spread = 1.0 / jnp.sqrt(jnp.mean(dev * dev, axis=-1, keepdims=True) + EPS)
        unit = dev * inv_spread
        mx[px, :] = unit
        inv[px, :] = jnp.broadcast_to(inv_spread, (width, LANE))
        nrm[px, :] = (unit * gain[...] + shift[...]).astype(BF)
        return carry

    lax.fori_loop(0, 8, norm, 0)

    r1_id = recvs.take(2)
    r1_cp = {}

    def weight_half(h):
        for p in range(h * quarter, (h + 1) * quarter):
            if p:
                g_cp[p][0].wait_recv()
                g_cp[p][1].wait_recv()
        if h == 0:
            own_ga.wait()
            own_gb.wait()
        for p in range(h * quarter, (h + 1) * quarter, 2):
            first, second = gb[p].astype(F32), gb[p + 1].astype(F32)
            at = pair_block(p)
            gm[at, 0:half_px, :] = jnp.where(low, first, pltpu.roll(second, LANE // 2, 1)).astype(BF)
            gm[at, half_px:, :] = jnp.where(low, pltpu.roll(first, LANE // 2, 1), second).astype(BF)

        def weight_part(j, carry):
            at = h * per_half + 2 * j
            g2 = jnp.concatenate([gm[at], gm[at + 1]], axis=1)
            lanes = pl.ds(pl.multiple_of(j * 2 * LANE, 2 * LANE), 2 * LANE)
            for i in range(chans // 256):
                part = lax.dot_general(
                    nrm[:, i * 256:(i + 1) * 256], g2, (((0,), (0,)), ((), ())), preferred_element_type=F32
                )
                wgp[h, 8 * i:8 * i + 8, :, :, lanes] = part.astype(BF).reshape(8, 2, 16, 2 * LANE)
            return carry

        lax.fori_loop(0, per_half // 2, weight_part, 0)
        r1_cp[h] = send(wgp.at[h, :, 1 - core], r1.at[h], r1_id + h, core_s, r)

    rp_id, rm_id = recvs.take(2 * plus), recvs.take(2 * minus)
    rp_cp, rm_cp = {}, {}

    def local_sum(h, xl_, z_):
        at = xl_ * nz + z_
        return wgp[h, at, core].astype(F32) + r1[h, at].astype(F32)

    def ring_r(t, h):
        if t == 0:
            r1_cp[h].wait_recv()
        if t < minus:
            if t > 0:
                rm_cp[t - 1, h].wait_recv()
            for xl_ in range(2):
                value = local_sum(h, xl_, zat(t - minus))
                if t > 0:
                    value = value + rm[t - 1, h, xl_].astype(F32)
                sm[t, h, xl_] = value.astype(BF)
            rm_cp[t, h] = send(sm.at[t, h], rm.at[t, h], rm_id + 2 * t + h, zm_s, r)
        if t < plus:
            if t > 0:
                rp_cp[t - 1, h].wait_recv()
            for xl_ in range(2):
                value = local_sum(h, xl_, zat(plus - t))
                if t > 0:
                    value = value + rp[t - 1, h, xl_].astype(F32)
                sp[t, h, xl_] = value.astype(BF)
            rp_cp[t, h] = send(sp.at[t, h], rp.at[t, h], rp_id + 2 * t + h, zp_s, r)

    r4_id = recvs.take(4 * ny)
    r4_cp = []

    def finish(h):
        rm_cp[minus - 1, h].wait_recv()
        rp_cp[plus - 1, h].wait_recv()
        for sub in range(2):
            xl_ = 1 - xl if sub else xl
            done = local_sum(h, xl_, z) + rm[minus - 1, h, xl_].astype(F32) + rp[plus - 1, h, xl_].astype(F32)
            for p in range(h * quarter, (h + 1) * quarter):
                f4[2 * p + sub, 0] = done[:, lanes_of(main_block(p) - h * per_half)]
                f4[2 * p + sub, 1] = done[:, lanes_of(pair_block(p) - h * per_half)]
        for p in range(h * quarter, (h + 1) * quarter):
            for sub in range(2):
                if p or sub:
                    at = 2 * p + sub
                    r4_cp.append(
                        send(f4.at[at], r4.at[at], r4_id + at, xlp_s if sub else s, row(yat(off[p]), xh))
                    )

    gn_id = recvs.take(chans // 256)
    gn_cp = []

    def grad_part(i):
        value = jnp.zeros((gm.shape[1], 256), F32)
        for j in range(blocks // 2):
            g2 = jnp.concatenate([gm[2 * j], gm[2 * j + 1]], axis=1)
            here = wall[16 * i:16 * i + 16, :, lanes_of(2 * j, 2)].reshape(256, 256)
            value = value + lax.dot_general(
                g2, here, (((1,), (1,)), ((), ())), preferred_element_type=F32
            )
        gnp[:, 256 * i:256 * i + 256] = value
        gns[i] = value.astype(BF)
        gn_cp.append(send(gns.at[i], gnr.at[i], gn_id + i, s, row(y, 1 - xh)))

    def norm_back(i, carry):
        px = pl.ds(pl.multiple_of(i * width, width), width)
        other = jnp.concatenate([gnr[j, px, :] for j in range(chans // 256)], axis=1)
        scaled = (gnp[px, :] + other.astype(F32)) * gain[...]
        unit = mx[px, :]
        first = jnp.mean(scaled, axis=-1, keepdims=True)
        second = jnp.mean(scaled * unit, axis=-1, keepdims=True)
        gmx[3 + i] = (inv[px, 0:1] * (scaled - first - unit * second)).astype(BF)
        return carry

    def expand_back(i, carry):
        at = 4 * xh + i
        line = 8 * y - 3 + at
        ok = (line >= 0) & (line < height_all) & (col_ids >= 0)
        xp[i, 8:8 + width, :] = jnp.where(ok, gmx[at].astype(F32), 0.0)
        return carry

    out_cols = lax.broadcasted_iota(jnp.int32, (width, LANE), 0)

    def put_out(out, lanes, value):
        ok = (out_cols < wid) & (8 * y + 4 * xh + out < height)
        ig[out, :, lanes] = jnp.where(ok, value, 0.0).astype(BF)

    def conv_back(lane, carry):
        conv(4, True, lane, put_out)
        return carry

    weight_half(0)
    ring_w_step(6)
    ring_r(0, 0)
    weight_half(1)
    for cp in wc_cp:
        cp.wait_recv()
    for i in range(chans // 256):
        grad_part(i)
    ring_r(0, 1)
    ring_r(1, 0)
    ring_r(1, 1)
    ring_r(2, 0)
    ring_r(2, 1)
    ring_r(3, 0)
    ring_r(3, 1)
    for cp in gn_cp:
        cp.wait_recv()
    lax.fori_loop(0, 8, norm_back, 0)
    hb_id = recvs.take()
    hb_cp = send(
        gmx.at[pl.ds(8 - 5 * xh, 3)], gmx.at[pl.ds(11 * xh, 3)], hb_id, s, row(yat(1 - 2 * xh), xh)
    )
    ring_r(4, 0)
    ring_r(4, 1)
    ring_r(5, 0)
    ring_r(5, 1)
    finish(0)
    finish(1)
    hb_cp.wait_recv()
    lax.fori_loop(0, 10, expand_back, 0)
    lax.fori_loop(0, chunks, conv_back, 0)
    for cp in r4_cp:
        cp.wait_recv()
    r4[0] = f4[0]
    main = r4[0, 0]
    tails = [r4[0, 1], r4[2, 1]]
    for at in range(1, 2 * ny):
        main = main + r4[at, 0]
        if at not in (0, 2):
            tails[(at // 2) % 2] = tails[(at // 2) % 2] + r4[at, 1]
    tail = tails[0] + pltpu.roll(tails[1], LANE // 2, 1)
    wg[:, 0:LANE] = main / images
    wg[:, LANE:] = tail[:, 0:LANE // 2] / images

    for cp in started:
        cp.wait_send()
    assert slots.count <= ssem.shape[0] and recvs.count <= rsem.shape[0]


def local(ny, nz, images, activations, cotangent, proj_weight, kernel_taps, ln_gain, ln_shift, heights, widths):
    rows_dev, width, chans = activations.shape[1:]
    height_all, hidden = cotangent.shape[1], cotangent.shape[3]
    blocks = ny + ny // 2
    px = 2 * rows_dev * width
    plus, minus = (nz - 1) // 2, nz // 2
    cols = blocks * LANE
    vmem = pltpu.VMEM
    out = pl.pallas_call(
        functools.partial(kernel_body, ny, nz, float(images)),
        out_shape=(
            pltpu.VMEM((rows_dev, width, chans), BF),
            pltpu.VMEM((16, hidden), F32),
        ),
        in_specs=[pl.BlockSpec(memory_space=pltpu.SMEM)] * 2
        + [pl.BlockSpec(memory_space=pl.ANY)] * 2
        + [pl.BlockSpec(memory_space=vmem)] * 4,
        out_specs=[pl.BlockSpec(memory_space=vmem)] * 2,
        scratch_shapes=[
            vmem((14, width, chans), BF),
            vmem((14, width + 16, chans), F32),
            vmem((56, chans), F32),
            vmem((px, chans), F32),
            vmem((px, LANE), F32),
            vmem((px, chans), BF),
            vmem((height_all, width, hidden), BF),
            vmem((ny, px, LANE), BF),
            vmem((ny, px // 2, LANE), BF),
            vmem((blocks, px, LANE), BF),
            vmem((ny, px // 2, LANE), BF),
            vmem((16, 2 * LANE), BF),
            vmem((2 * ny, 16, 2 * LANE), BF),
            vmem((4 * nz, 16, cols), BF),
            vmem((2, 2 * nz, 2, 16, cols // 2), BF),
            vmem((2, 2 * nz, 16, cols // 2), BF),
            vmem((plus, 2, 2, 16, cols // 2), BF),
            vmem((minus, 2, 2, 16, cols // 2), BF),
            vmem((plus, 2, 2, 16, cols // 2), BF),
            vmem((minus, 2, 2, 16, cols // 2), BF),
            vmem((2 * ny, 2, 16, LANE), F32),
            vmem((2 * ny, 2, 16, LANE), F32),
            vmem((px, chans), F32),
            vmem((chans // 256, px, 256), BF),
            vmem((chans // 256, px, 256), BF),
            vmem((14, width, chans), BF),
            vmem((1, chans), F32),
            vmem((1, chans), F32),
            pltpu.SemaphoreType.DMA((192,)),
            pltpu.SemaphoreType.DMA((192,)),
            pltpu.SemaphoreType.DMA((3,)),
        ],
        compiler_params=pltpu.CompilerParams(
            collective_id=0, has_side_effects=True, vmem_limit_bytes=60 * 1024 * 1024
        ),
    )(
        heights, widths, activations[0], cotangent[0], proj_weight, kernel_taps,
        ln_gain, ln_shift,
    )
    return out[0][None], out[1]


def solution(mesh):
    ny = mesh.shape["rows"] // 2
    nz = mesh.shape["section"] // 4
    in_specs = (
        P("section", "rows", None, None),
        P("section", None, None, "rows"),
        P("section", "rows"),
        P(),
        P(),
        P(),
        P("section"),
        P("section"),
    )
    out_specs = (P("section", "rows", None, None), P("section", "rows"))
    body = functools.partial(local, ny, nz, mesh.shape["section"])
    return jax.shard_map(body, mesh=mesh, in_specs=in_specs, out_specs=out_specs, check_vma=False)
```
